32 devices in a mesh: lon: 4 (over y, core), lat: 4 (over z), dp: 2 (over x).
Axes of the slice: x: 2, y: 2, z: 4, core: 2. Of those that a mesh axis runs over, the one named last changes fastest.
Arguments:
- tokens: bfloat16 [2, 2, 24, 48, 192], P('dp', None, 'lat', 'lon'), may hold values from -6 to 6
- grad_out: bfloat16 [2, 2, 24, 48, 192], P('dp', None, 'lat', 'lon'), may hold values from -6 to 6
- qkv_weight: bfloat16 [576, 192], P('dp'), may hold values from -0.4375 to 0.4375
- proj_weight: bfloat16 [192, 192], P('dp'), may hold values from -0.4375 to 0.4375
- norm_gain: bfloat16 [192], P('dp'), may hold values from 0.5 to 1.5
- bias_table: float32 [4, 6, 3312], P('lat'), may hold values from -2.5 to 402.5
Outputs:
- grad_tokens: bfloat16 [2, 2, 24, 48, 192], P('dp', None, 'lat', 'lon')
- grad_qkv_weight: float32 [576, 192], P('dp')
- grad_proj_weight: float32 [192, 192], P('dp')
- grad_norm_gain: float32 [192], P('dp')
- grad_bias_table: float32 [4, 6, 3312], P('lat')
The draws below stay inside these ranges and needn't reach their ends.
All inputs are finite; a program needn't handle non-finite values.
Results may differ from the reference program's by a relative error of at most 0.015.
Values may be sent and summed in bfloat16 or wider, within the bound.
No kernel may reach another device: no remote copies, remote signals or barrier semaphores. Data moves between devices by JAX's collectives and lax.ppermute only.
A program may use at most 64 MiB of HBM per device.

```python
import math
import jax
import jax.numpy as jnp
from jax import lax

C = 192
H = 6
HD = 32
WZ = 2
WA = 6
WL = 12
SA = 3
SO = 6
WT = 144
POS = 3312
ZL = 2
MEMBERS = 2
LAT = 24
LON = 48
NTYPE = 4


def draw_bias_table(key, part):
    base = jnp.clip(0.5 * jax.random.normal(key, (NTYPE, H, POS), jnp.float32), -2.5, 2.5)
    return base


def with_spikes(drawn, key, source, target, blocks, factor):
    def block_of(dim):
        return (jnp.arange(drawn.shape[dim]) // (drawn.shape[dim] // blocks)).reshape((-1,) + (1,) * (drawn.ndim - 1 - dim))

    near = jax.random.permutation(key, blocks)[block_of(target)]
    far = (block_of(target) + blocks // 2) % blocks
    return jnp.where((block_of(source) == near) | (block_of(source) == far), factor * drawn, drawn)


def steps_of(stream_key, extent, pieces, smallest, top_value):
    factor_of = 1.0
    for dim, blocks in pieces:
        heights = jax.random.uniform(jax.random.fold_in(jax.random.fold_in(stream_key, 6), dim), (blocks,), jnp.float32, smallest / len(pieces), top_value / len(pieces))
        factor_of = factor_of * jnp.repeat(jnp.exp(heights), extent[dim] // blocks).reshape((-1,) + (1,) * (len(extent) - 1 - dim))
    return factor_of


def bell_draw(rng, dims, deviation, most, shards=(), held_as=jnp.bfloat16):
    drawn = jax.random.normal(rng, dims, jnp.float32) * deviation
    if len(shards) > 0:
        drawn = steps_of(rng, dims, shards, -0.22, 0.18) * drawn
    return jnp.clip(drawn, min=-most, max=most).astype(held_as)


def gaussian_with(rng, extent, deviation, most, cuts, heavy, kind=jnp.bfloat16):
    values = deviation * jax.random.normal(rng, extent, jnp.float32)
    if cuts:
        values = values * steps_of(rng, extent, cuts, -0.22, 0.18)
    return jnp.clip(with_spikes(values, jax.random.fold_in(rng, 3), *heavy), -most, most).astype(kind)


def setup_inputs(seed: int = 0) -> dict:
    keys = jax.random.split(jax.random.key(seed), 7)
    return {
        "tokens": bell_draw(keys[0], (MEMBERS, ZL, LAT, LON, C), 1.0, 6.0, ((0, 2), (2, 4), (3, 4))),
        "grad_out": gaussian_with(keys[1], (MEMBERS, ZL, LAT, LON, C), 1.0, 6.0, ((0, 2), (2, 4), (3, 4)), (0, 4, 2, 2.0)),
        "qkv_weight": bell_draw(keys[2], (3 * C, C), C ** -0.5, 0.4375, ((0, 2),)),
        "proj_weight": bell_draw(keys[3], (C, C), C ** -0.5, 0.4375, ((0, 2),)),
        "norm_gain": jnp.clip(1.0 + 0.1 * jax.random.normal(keys[4], (C,), jnp.float32), 0.5, 1.5).astype(jnp.bfloat16),
        "bias_table": draw_bias_table(jax.random.fold_in(keys[6], 71), 0),
    }


EPS = 1e-05
MASKED = -1e+30

def offsets_table():
    first = jnp.arange(WL)[:, None, None]
    second = jnp.arange(WL)[None, :, None]
    offset = jnp.arange(2 * WL - 1)[None, None, :]
    return (offset == first - second + WL - 1).astype(jnp.float32)

def spread_bias(table, onehot):
    window_rows = WZ * WA
    shaped = table.reshape(table.shape[0], H, window_rows, window_rows, 2 * WL - 1)
    spread = jnp.einsum('ghabr,uvr->ghaubv', shaped, onehot, precision=lax.Precision.HIGHEST)
    return spread.reshape(table.shape[0], H, WT, WT)

def gather_bias(grad_full, onehot):
    window_rows = WZ * WA
    shaped = grad_full.reshape(grad_full.shape[0], H, window_rows, WL, window_rows, WL)
    folded = jnp.einsum('ghaubv,uvr->ghabr', shaped, onehot, precision=lax.Precision.HIGHEST)
    return folded.reshape(grad_full.shape[0], H, POS)

def to_windows(grid, lat_rows, lon_cols):
    members, levels, channels = (grid.shape[0], grid.shape[1], grid.shape[4])
    lat_types = lat_rows // WA
    lon_windows = lon_cols // WL
    parts = grid.reshape(members, levels, lat_types, WA, lon_windows, WL, channels)
    parts = parts.transpose(2, 0, 4, 1, 3, 5, 6)
    return parts.reshape(lat_types, members * lon_windows, WT, channels)

def lift(value):
    return lax.optimization_barrier(value).astype(jnp.float32)

def window_grads(window_x, window_dy, window_flag, table, qkv_weight, proj_weight, norm_gain, onehot):
    groups, count = (window_x.shape[0], window_x.shape[1])
    flat_x = window_x.reshape(-1, C).astype(jnp.float32)
    average = lax.optimization_barrier(jnp.mean(flat_x, axis=-1, keepdims=True))
    centred = flat_x - average
    variance = lax.optimization_barrier(jnp.mean(centred * centred, axis=-1, keepdims=True))
    inverse = lax.rsqrt(variance + EPS)
    unit = centred * inverse
    gain_value = norm_gain.astype(jnp.float32)
    normed = (unit * gain_value).astype(jnp.bfloat16)
    projected = jnp.dot(normed, qkv_weight.T, preferred_element_type=jnp.float32).astype(jnp.bfloat16)
    split = lift(projected).reshape(groups, count, WT, 3, H, HD)
    queries = split[:, :, :, 0]
    key_part = split[:, :, :, 1]
    values = split[:, :, :, 2]
    head_scale = 1.0 / math.sqrt(HD)
    bias_full = spread_bias(table, onehot)
    scores = jnp.einsum('gwqhd,gwkhd->gwhqk', queries, key_part) * head_scale
    scores = scores + bias_full[:, None]
    allowed = window_flag[:, :, None, :, None] == window_flag[:, :, None, None, :]
    scores = jnp.where(allowed, scores, MASKED)
    highest = lax.optimization_barrier(jnp.max(scores, axis=-1, keepdims=True))
    expo = jnp.exp(scores - highest)
    probs = expo / lax.optimization_barrier(jnp.sum(expo, axis=-1, keepdims=True))
    probs_low = lift(probs.astype(jnp.bfloat16))
    attended = jnp.einsum('gwhqk,gwkhd->gwqhd', probs_low, values).astype(jnp.bfloat16).reshape(-1, C)
    flat_dy = window_dy.reshape(-1, C)
    grad_proj = jnp.dot(flat_dy.T, attended, preferred_element_type=jnp.float32)
    grad_att = jnp.dot(flat_dy, proj_weight, preferred_element_type=jnp.float32).astype(jnp.bfloat16)
    grad_att = lift(grad_att).reshape(groups, count, WT, H, HD)
    grad_probs = jnp.einsum('gwqhd,gwkhd->gwhqk', grad_att, values)
    grad_values = jnp.einsum('gwhqk,gwqhd->gwkhd', probs_low, grad_att)
    grad_scores = probs * (grad_probs - lax.optimization_barrier(jnp.sum(probs * grad_probs, axis=-1, keepdims=True)))
    scores_low = lift(grad_scores.astype(jnp.bfloat16))
    grad_queries = jnp.einsum('gwhqk,gwkhd->gwqhd', scores_low, key_part) * head_scale
    grad_keys = jnp.einsum('gwhqk,gwqhd->gwkhd', scores_low, queries) * head_scale
    grad_qkv = jnp.stack([grad_queries, grad_keys, grad_values], axis=3).reshape(-1, 3 * C).astype(jnp.bfloat16)
    grad_qkv_w = jnp.dot(grad_qkv.T, normed, preferred_element_type=jnp.float32)
    grad_normed = jnp.dot(grad_qkv, qkv_weight, preferred_element_type=jnp.float32)
    grad_gain = lax.optimization_barrier(jnp.sum(grad_normed * unit, axis=0))
    scaled = grad_normed * gain_value
    grad_x = inverse * (scaled - lax.optimization_barrier(jnp.mean(scaled, axis=-1, keepdims=True)) - unit * lax.optimization_barrier(jnp.mean(scaled * unit, axis=-1, keepdims=True)))
    grad_table = gather_bias(lax.optimization_barrier(jnp.sum(grad_scores, axis=1)), onehot)
    return (grad_x.reshape(groups, count, WT, C), grad_qkv_w, grad_proj, grad_gain, grad_table)

def reference(tokens, grad_out, qkv_weight, proj_weight, norm_gain, bias_table):
    onehot = offsets_table()
    shifted = jnp.roll(tokens, (-SA, -SO), axis=(2, 3))
    shifted_dy = jnp.roll(grad_out, (-SA, -SO), axis=(2, 3))
    wrapped = jnp.arange(LAT) >= LAT - SA

    def one_band(index):
        member = (index // NTYPE).astype(jnp.int32)
        band = (index % NTYPE).astype(jnp.int32)
        start = (band * WA).astype(jnp.int32)
        zero = jnp.int32(0)
        piece_x = lax.dynamic_slice(shifted, (member, zero, start, zero, zero), (1, ZL, WA, LON, C))
        piece_dy = lax.dynamic_slice(shifted_dy, (member, zero, start, zero, zero), (1, ZL, WA, LON, C))
        piece_flag = lax.dynamic_slice(wrapped, (start,), (WA,))
        flag_grid = jnp.broadcast_to(piece_flag[None, None, :, None, None], (1, ZL, WA, LON, 1))
        table = lax.dynamic_slice_in_dim(bias_table, band, 1, 0)
        return window_grads(to_windows(piece_x, WA, LON), to_windows(piece_dy, WA, LON), to_windows(flag_grid, WA, LON)[..., 0], table, qkv_weight, proj_weight, norm_gain, onehot)
    results = lax.map(one_band, jnp.arange(MEMBERS * NTYPE, dtype=jnp.int32))
    grad_windows = results[0].reshape(MEMBERS, NTYPE, LON // WL, ZL, WA, WL, C)
    grad_shifted = grad_windows.transpose(0, 3, 1, 4, 2, 5, 6).reshape(MEMBERS, ZL, LAT, LON, C)
    restored = jnp.roll(grad_shifted, (SA, SO), axis=(2, 3))
    grad_tokens = (grad_out.astype(jnp.float32) + restored).astype(jnp.bfloat16)
    grad_qkv_weight = lax.optimization_barrier(jnp.sum(results[1], axis=0))
    grad_proj_weight = lax.optimization_barrier(jnp.sum(results[2], axis=0))
    grad_norm_gain = lax.optimization_barrier(jnp.sum(results[3], axis=0))
    grad_bias_table = lax.optimization_barrier(jnp.sum(results[4].reshape(MEMBERS, NTYPE, H, POS), axis=0))
    return (grad_tokens, grad_qkv_weight, grad_proj_weight, grad_norm_gain, grad_bias_table)
```

```python
import functools
import math

import jax
import jax.numpy as jnp
import numpy as np
from jax import lax
from jax.experimental import pallas as pl
from jax.experimental.pallas import tpu as pltpu
from jax.sharding import PartitionSpec as P

C = 192
H = 6
HD = 32
WZ = 2
WA = 6
WL = 12
SA = 3
SO = 6
WT = 144
POS = 3312
EPS = 1e-05
MASKED = -1e30

ROWS = WZ * WA
SPAN = 2 * WL - 1
QUAD = WZ * SA * 8
HALF = ROWS // 2 * SPAN
WIDE = 256
EXT = 2 * H * ROWS + 8
BF = jnp.bfloat16
F32 = jnp.float32
VMEM = pl.BlockSpec(memory_space=pltpu.VMEM)
SMEM = pl.BlockSpec(memory_space=pltpu.SMEM)


def token_order():
    order = np.zeros((WT, 4 * QUAD), np.float32)
    for z in range(WZ):
        for a in range(WA):
            for o in range(WL):
                south, east = a >= SA, o >= SO
                quadrant = 2 * south + east
                column = o - SO if east else o + 2
                row = (z * SA + a % SA) * 8 + column
                order[(z * WA + a) * WL + o, quadrant * QUAD + row] = 1.0
    return order


def matmul(a, b):
    return lax.dot_general(a, b, (((1,), (0,)), ((), ())), preferred_element_type=F32)


def matmul_t(a, b):
    return lax.dot_general(a, b, (((1,), (1,)), ((), ())), preferred_element_type=F32)


def over_12(index):
    return lax.shift_right_logical(index * 5462, 16)


def pack_kernel(tok, dy, east, south, corner):
    def strip(ref, rows, cols):
        part = ref[:, rows : rows + SA].astype(F32)
        return part[:, :, cols : cols + 8].reshape(QUAD, C).astype(BF)

    for index, ref in enumerate((tok, dy)):
        at = slice(index * QUAD, (index + 1) * QUAD)
        east[at] = strip(ref, SA, 0)
        south[at] = strip(ref, 0, 4)
        corner[at] = strip(ref, 0, 0)


def offsets(height, width, half):
    row = lax.broadcasted_iota(jnp.int32, (height, width), 0)
    col = lax.broadcasted_iota(jnp.int32, (height, width), 1)
    block = over_12(col)
    return row, block * SPAN - (col - block * WL) + WL - 1 - half


def bias_kernel(place, table, out):
    values = table[...]
    high = values.astype(BF)
    rest = values - high.astype(F32)
    middle = rest.astype(BF)
    low = (rest - middle.astype(F32)).astype(BF)
    stacked = jnp.concatenate([high, middle, low], axis=0)
    row, target = offsets(ROWS * SPAN, WIDE, 0)
    count = H * ROWS
    here = lax.broadcasted_iota(jnp.int32, (count, WIDE), 0)
    here = here - over_12(here) * ROWS
    there = over_12(lax.broadcasted_iota(jnp.int32, (count, WIDE), 1))

    def wrapped(index):
        return jnp.where(index >= WA, index - WA, index) >= SA

    crossing = jnp.logical_and(wrapped(here) != wrapped(there), place[2] > 0)
    for u in range(WL):
        onehot = jnp.where(row == target + u, 1.0, 0.0).astype(BF)
        spread = matmul(stacked, onehot)
        spread = spread[:count] + spread[count : 2 * count] + spread[2 * count :]
        spread = jnp.where(crossing, MASKED, spread)
        out[0, pl.ds(u, count, stride=WL), :] = spread[:, :128]
        out[1, pl.ds(u, count, stride=WL), :] = spread[:, 128:]


def main_kernel(
    parts, place, tok, dy, east, south, corner, bias, order, order_t, *refs
):
    dense = refs[:parts]
    send, keep, extra, quads, qkv_w, proj_w, sums, scores_grad = refs[parts:]
    n_qkv, n_proj = 3 * C // parts, C // parts
    gain = None
    for k in range(parts):
        at = lax.rem(place[0] + k, parts)
        qkv_w[pl.ds(pl.multiple_of(at * n_qkv, 16), n_qkv), :] = dense[k][:n_qkv]
        proj_w[pl.ds(pl.multiple_of(at * n_proj, 16), n_proj), :] = dense[k][n_qkv : n_qkv + n_proj]
        term = dense[k][n_qkv + n_proj : n_qkv + n_proj + 8].astype(F32)[:1]
        gain = term if gain is None else gain + term

    def own(ref):
        part = ref[:, SA:].astype(F32)
        return part[:, :, 4:12].reshape(QUAD, C).astype(BF)

    def window(ref, index):
        at = slice(index * QUAD, (index + 1) * QUAD)
        return jnp.concatenate([own(ref), east[at], south[at], corner[at]], axis=0)

    x = matmul(order[...], window(tok, 0))
    dyw = matmul(order[...], window(dy, 1)).astype(BF)
    average = jnp.sum(x, axis=-1, keepdims=True) * (1.0 / C)
    centred = x - average
    variance = jnp.sum(centred * centred, axis=-1, keepdims=True) * (1.0 / C)
    inverse = lax.rsqrt(variance + EPS)
    unit = centred * inverse
    normed = (unit * gain).astype(BF)
    qkv_t = matmul_t(qkv_w[...], normed).astype(BF)
    query = matmul_t(normed, qkv_w[:C]).astype(BF)
    grad_att32 = matmul(dyw, proj_w[...]).astype(BF).astype(F32)
    grad_att = grad_att32.astype(BF)
    grad_att_t = grad_att32.T.astype(BF)
    dy_t = dyw.astype(F32).T.astype(BF)
    scale = 1.0 / math.sqrt(HD)

    def alone(part, head):
        pieces = []
        if head:
            pieces.append(jnp.zeros((head * HD, WT), BF))
        pieces.append(part)
        if head < H - 1:
            pieces.append(jnp.zeros(((H - 1 - head) * HD, WT), BF))
        return jnp.concatenate(pieces, axis=0)

    def both(ref, at):
        rows = slice(at, at + WT)
        return jnp.concatenate([ref[0, rows], ref[1, rows, : WT - 128]], axis=1)

    attended_t, grad_q, grad_k, grad_v = [], [], [], []
    for head in range(H):
        at = head * HD
        q_t = qkv_t[at : at + HD]
        k_t = qkv_t[C + at : C + at + HD]
        v_t = qkv_t[2 * C + at : 2 * C + at + HD]
        scores = matmul(query, alone(k_t, head)) * scale + both(bias, head * WT)
        expo = jnp.exp(scores - jnp.max(scores, axis=-1, keepdims=True))
        probs = expo * (1.0 / jnp.sum(expo, axis=-1, keepdims=True))
        probs_low = probs.astype(BF)
        attended_t.append(matmul_t(v_t, probs_low))
        grad_probs = matmul(grad_att, alone(v_t, head))
        grad_v.append(matmul(grad_att_t[at : at + HD], probs_low))
        mean = jnp.sum(probs * grad_probs, axis=-1, keepdims=True)
        grad_scores = probs * (grad_probs - mean)
        scores_grad[0, head * WT : (head + 1) * WT] = grad_scores[:, :128]
        scores_grad[1, head * WT : (head + 1) * WT, : WT - 128] = grad_scores[:, 128:]
        scores_low = grad_scores.astype(BF)
        grad_q.append(matmul_t(k_t, scores_low) * scale)
        grad_k.append(matmul(q_t, scores_low) * scale)
    grad_qkv_t32 = jnp.concatenate(grad_q + grad_k + grad_v, axis=0)
    grad_qkv_t = grad_qkv_t32.astype(BF)
    grad_qkv_w = matmul(grad_qkv_t, normed)
    grad_proj = matmul_t(dy_t, jnp.concatenate(attended_t, axis=0).astype(BF))
    each = n_qkv + n_proj
    for k in range(parts):
        sums[k * each : k * each + n_qkv] = grad_qkv_w[k * n_qkv : (k + 1) * n_qkv]
        sums[k * each + n_qkv : (k + 1) * each] = grad_proj[k * n_proj : (k + 1) * n_proj]
    for k in range(parts):
        mine = k * each + place[1] * (each // 2)
        other = k * each + (1 - place[1]) * (each // 2)
        rows = slice(k * (each // 2), (k + 1) * (each // 2))
        keep[rows] = sums[pl.ds(pl.multiple_of(mine, 16), each // 2), :]
        send[rows] = sums[pl.ds(pl.multiple_of(other, 16), each // 2), :].astype(BF)

    grad_qkv = grad_qkv_t32.T.astype(BF)
    grad_normed = matmul(grad_qkv, qkv_w[...])
    grad_gain = jnp.sum(grad_normed * unit, axis=0, keepdims=True)
    scaled = grad_normed * gain
    first = jnp.sum(scaled, axis=-1, keepdims=True) * (1.0 / C)
    second = jnp.sum(scaled * unit, axis=-1, keepdims=True) * (1.0 / C)
    grad_x = inverse * (scaled - first - unit * second)
    quads[...] = matmul(order_t[...], grad_x.astype(BF)).astype(BF)

    count = H * ROWS
    for half in range(2):
        row, target = offsets(C, WT, half * HALF)
        target = jnp.where(row < HALF, target, -WT)
        total = jnp.zeros((count, C), F32)
        for u in range(WL):
            onehot = jnp.where(row == target + u, 1.0, 0.0).astype(BF)
            rows = pl.ds(u, count, stride=WL)
            wide = jnp.concatenate(
                [scores_grad[0, rows, :], scores_grad[1, rows, :][:, : WT - 128]], axis=1
            )
            total += matmul_t(wide.astype(BF), onehot)
        extra[half * count : (half + 1) * count] = total.astype(BF)
    extra[2 * count : EXT] = jnp.broadcast_to(grad_gain, (8, C)).astype(BF)


def finish_kernel(dy, quad, south, lon_halo, out):
    def low(ref, at):
        value = ref[at : at + QUAD].astype(F32).reshape(WZ, SA, 8, C)
        return jnp.concatenate([value, jnp.zeros((WZ, SA, 4, C), F32)], axis=2)

    def high(ref, at):
        value = ref[at : at + QUAD].astype(F32).reshape(WZ, SA, 8, C)
        return jnp.concatenate([jnp.zeros((WZ, SA, 4, C), F32), value], axis=2)

    upper = dy[:, :SA].astype(F32) + low(lon_halo, QUAD) + high(south, 0)
    lower = dy[:, SA:].astype(F32) + low(lon_halo, 0) + high(quad, 0)
    out[:, :SA] = upper.astype(BF)
    out[:, SA:] = lower.astype(BF)


def call(kernel, outs, scratch=(), specs=None, flops=1000000, nbytes=1000000):
    return pl.pallas_call(
        kernel,
        out_shape=outs,
        in_specs=specs,
        out_specs=jax.tree.map(lambda _: VMEM, outs),
        scratch_shapes=list(scratch),
        compiler_params=pltpu.CompilerParams(vmem_limit_bytes=40 << 20),
        cost_estimate=pl.CostEstimate(flops=flops, bytes_accessed=nbytes, transcendentals=0),
    )


def shaped(rows, cols, dtype):
    return jax.ShapeDtypeStruct((rows, cols), dtype)


def exchanged(value, axis, flip):
    count = lax.axis_size(axis)
    return lax.ppermute(value, axis, [(i, i ^ flip) for i in range(count)])


def passed_along(value, axis, steps):
    count = lax.axis_size(axis)
    return lax.ppermute(value, axis, [(i, (i + steps) % count) for i in range(count)])


def passed_diagonally(value, steps):
    rows, cols = lax.axis_size("lon"), lax.axis_size("lat")
    pairs = [
        (i * cols + j, ((i + steps) % rows) * cols + (j + steps) % cols)
        for i in range(rows)
        for j in range(cols)
    ]
    return lax.ppermute(value, ("lon", "lat"), pairs)


def body(tokens, grad_out, qkv_weight, proj_weight, norm_gain, bias_table):
    parts = lax.axis_size("dp")
    dp, lon, lat = lax.axis_index("dp"), lax.axis_index("lon"), lax.axis_index("lat")
    lon_count, lat_count = lax.axis_size("lon"), lax.axis_size("lat")
    n_qkv, n_proj = 3 * C // parts, C // parts
    each = n_qkv + n_proj
    half = each // 2
    side = (lon ^ (lon >> 1)) & 1
    place = jnp.stack([dp, side, lat == lat_count - 1]).astype(jnp.int32)
    tok = tokens.reshape(WZ, WA, WL, C)
    dy = grad_out.reshape(WZ, WA, WL, C)

    gain_row = lax.dynamic_update_slice(jnp.zeros((C,), BF), norm_gain, (dp * n_proj,))
    dense = jnp.concatenate(
        [qkv_weight, proj_weight, jnp.broadcast_to(gain_row, (8, C))], axis=0
    )
    strips = [shaped(2 * QUAD, C, BF)] * 3
    east, south, corner = call(pack_kernel, strips, specs=[VMEM] * 2)(tok, dy)
    gathered = [dense] + [passed_along(dense, "dp", -k) for k in range(1, parts)]
    east = passed_along(east, "lon", -1)
    south = passed_along(south, "lat", -1)
    corner = passed_diagonally(corner, -1)
    bias = call(bias_kernel, jax.ShapeDtypeStruct((2, H * WT, 128), F32), specs=[SMEM, VMEM], flops=200000000)(
        place, bias_table.reshape(H * ROWS, ROWS * SPAN)
    )
    order = token_order()
    outs = [
        shaped(parts * half, C, BF),
        shaped(parts * half, C, F32),
        shaped(EXT, C, BF),
        shaped(4 * QUAD, C, BF),
    ]
    scratch = [
        pltpu.VMEM((3 * C, C), BF),
        pltpu.VMEM((C, C), BF),
        pltpu.VMEM((4 * C, C), F32),
        pltpu.VMEM((2, H * WT, 128), F32),
    ]
    send, keep, extra, quads = call(
        functools.partial(main_kernel, parts), outs, scratch, specs=[SMEM] + [VMEM] * (8 + parts)
    )(
        place, tok, dy, east, south, corner, bias,
        jnp.asarray(order, BF), jnp.asarray(order.T, BF), *gathered,
    )
    if (lon_count, lat_count, parts) == (4, 4, 2):
        first = keep + exchanged(send, "lon", 1).astype(F32)
        mine = lax.dynamic_slice_in_dim(first, dp * half, half)
        theirs = lax.dynamic_slice_in_dim(first, (1 - dp) * half, half).astype(BF)
        got = exchanged(jnp.concatenate([theirs, extra]), "dp", 1)
        dense_sum = (mine + got[:half].astype(F32)).astype(BF)
        extra = extra + got[half:]
        dense_sum = jnp.concatenate([dense_sum, extra[2 * H * ROWS :]])
        extra = extra[: 2 * H * ROWS]
        full = half + 8
        south_quads = quads[2 * QUAD :]
        got = exchanged(jnp.concatenate([dense_sum, south_quads]), "lat", 1)
        dense_sum = dense_sum + got[:full]
        south_halo = got[full:]
        got = exchanged(jnp.concatenate([dense_sum, south_quads]), "lat", 3)
        dense_sum = dense_sum + got[:full]
        south_halo = jnp.where(lat % 2 == 1, south_halo, got[full:])
        east_quads = jnp.concatenate([quads[QUAD : 2 * QUAD], south_halo[QUAD:]])
        got = exchanged(jnp.concatenate([dense_sum, extra, east_quads]), "lon", 3)
        dense_sum = dense_sum + got[:full]
        extra = extra + got[full : half + EXT]
        east_halo = got[half + EXT :]
        got = exchanged(jnp.concatenate([dense_sum, extra, east_quads]), "lon", 1)
        extra = extra.astype(F32) + got[full : half + EXT].astype(F32)
        east_halo = jnp.where(lon % 2 == 1, got[half + EXT :], east_halo)
        gain_sum = dense_sum[half].astype(F32) + got[half].astype(F32)
        dense_sum = dense_sum[:half]
        gain_sum = lax.dynamic_slice_in_dim(gain_sum, dp * n_proj, n_proj)
        total = jnp.where(
            side == 0,
            jnp.concatenate([dense_sum, got[:half]]),
            jnp.concatenate([got[:half], dense_sum]),
        ).astype(F32)
    else:
        paired = jnp.stack([keep.reshape(parts, half, C), send.reshape(parts, half, C).astype(F32)])
        paired = jnp.where(side == 0, paired, paired[::-1])
        dense_sum = paired.transpose(1, 0, 2, 3).reshape(parts * each, C)
        dense_sum = lax.psum(dense_sum, ("lon", "lat"))
        total = lax.psum_scatter(dense_sum, "dp", scatter_dimension=0, tiled=True)
        extra = extra.astype(F32)
        gain_sum = lax.psum(extra[2 * H * ROWS], ("lon", "lat"))
        gain_sum = lax.psum_scatter(gain_sum, "dp", scatter_dimension=0, tiled=True)
        extra = lax.psum(extra, ("lon", "dp"))
        south_halo = passed_along(quads[2 * QUAD :], "lat", 1)
        east_halo = passed_along(
            jnp.concatenate([quads[QUAD : 2 * QUAD], south_halo[QUAD:]]), "lon", 1
        )
    count = H * ROWS
    table = jnp.concatenate([extra[:count, :HALF], extra[count : 2 * count, :HALF]], axis=1)
    grad_tokens = call(
        finish_kernel, jax.ShapeDtypeStruct((WZ, WA, WL, C), BF), specs=[VMEM] * 4
    )(dy, quads, south_halo, east_halo)
    return (
        grad_tokens.reshape(tokens.shape),
        total[:n_qkv],
        total[n_qkv:],
        gain_sum,
        table.reshape(1, H, POS),
    )


def solution(mesh):
    spec = P("dp", None, "lat", "lon", None)
    return jax.shard_map(
        body,
        mesh=mesh,
        in_specs=(spec, spec, P("dp", None), P("dp", None), P("dp"), P("lat", None, None)),
        out_specs=(spec, P("dp", None), P("dp", None), P("dp"), P("lat", None, None)),
        check_vma=False,
    )
```

```python
import functools
import math

import jax
import jax.numpy as jnp
import numpy as np
from jax import lax
from jax.experimental import pallas as pl
from jax.experimental.pallas import tpu as pltpu
from jax.sharding import PartitionSpec as P

C = 192
H = 6
HD = 32
WZ = 2
WA = 6
WL = 12
SA = 3
SO = 6
WT = 144
POS = 3312
EPS = 1e-05
MASKED = -1e30

ROWS = WZ * WA
SPAN = 2 * WL - 1
QUAD = WZ * SA * 8
WIDE = 256
LEAD = 11 * SPAN
HALO = 3 * QUAD // 2
TABLE = H * ROWS + 16
BF = jnp.bfloat16
F32 = jnp.float32
VMEM = pl.BlockSpec(memory_space=pltpu.VMEM)


def dp_index():
    return lax.axis_index("dp")


def side_index():
    column = lax.axis_index("lon")
    return lax.rem(column + lax.div(column, 2), 2)


def last_row():
    return lax.axis_index("lat") == lax.axis_size("lat") - 1


def token_order():
    order = np.zeros((WT, 4 * QUAD), np.float32)
    for z in range(WZ):
        for a in range(WA):
            for o in range(WL):
                south, east = a >= SA, o >= SO
                quadrant = 2 * south + east
                column = o - SO if east else o + 2
                row = (z * SA + a % SA) * 8 + column
                order[(z * WA + a) * WL + o, quadrant * QUAD + row] = 1.0
    return order


def matmul(a, b):
    return lax.dot_general(a, b, (((1,), (0,)), ((), ())), preferred_element_type=F32)


def matmul_t(a, b):
    return lax.dot_general(a, b, (((1,), (1,)), ((), ())), preferred_element_type=F32)


def over_12(index):
    return lax.shift_right_logical(index * 5462, 16)


def spread_lanes(row, position, parts):
    width = row.shape[1]
    full = jnp.zeros((1, C), F32)
    for k in range(parts):
        pieces = [row]
        if k:
            pieces.insert(0, jnp.zeros((1, k * width), F32))
        if k < parts - 1:
            pieces.append(jnp.zeros((1, (parts - 1 - k) * width), F32))
        full = jnp.where(position == k, jnp.concatenate(pieces, axis=1), full)
    return full


def pack_kernel(parts, tok, dy, qkv, proj, gain, dense, east, south, corner):
    n_qkv, n_proj = 3 * C // parts, C // parts
    dense[:n_qkv] = qkv[...]
    dense[n_qkv : n_qkv + n_proj] = proj[...]
    row = spread_lanes(gain[...].astype(F32), dp_index(), parts)
    dense[n_qkv + n_proj :] = jnp.broadcast_to(row, (16, C)).astype(BF)

    def strip(ref, rows, cols):
        part = ref[:, rows : rows + SA].astype(F32)
        return part[:, :, cols : cols + 8].reshape(QUAD, C).astype(BF)

    for index, ref in enumerate((tok, dy)):
        at = slice(index * QUAD, (index + 1) * QUAD)
        east[at] = strip(ref, SA, 0)
        south[at] = strip(ref, 0, 4)
        corner[at] = strip(ref, 0, 0)


def folded(value):
    rows = value.shape[0]
    top, tail = value[: 3 * rows // 4], value[3 * rows // 4 :]
    side = jnp.concatenate([tail[:, at : at + 64] for at in (0, 64, 128)], axis=0)
    return jnp.concatenate([top, side], axis=1)


def unfolded(value):
    rows = value.shape[0] // 3
    side = value[:, C:]
    tail = jnp.concatenate([side[k * rows : (k + 1) * rows] for k in range(3)], axis=1)
    return jnp.concatenate([value[:, :C], tail], axis=0)


def offsets(height, width, half):
    row = lax.broadcasted_iota(jnp.int32, (height, width), 0)
    col = lax.broadcasted_iota(jnp.int32, (height, width), 1)
    block = over_12(col)
    return row, block * SPAN - (col - block * WL) + WL - 1 - half


def bias_kernel(table, out):
    values = table[...]
    high = values.astype(BF)
    rest = values - high.astype(F32)
    middle = rest.astype(BF)
    low = (rest - middle.astype(F32)).astype(BF)
    stacked = jnp.concatenate([high, middle, low], axis=0)
    row, target = offsets(ROWS * SPAN, WIDE, 0)
    count = H * ROWS
    here = lax.broadcasted_iota(jnp.int32, (count, WIDE), 0)
    here = here - over_12(here) * ROWS
    there = over_12(lax.broadcasted_iota(jnp.int32, (count, WIDE), 1))

    def wrapped(index):
        return jnp.where(index >= WA, index - WA, index) >= SA

    crossing = jnp.logical_and(wrapped(here) != wrapped(there), last_row())
    for u in range(WL):
        onehot = jnp.where(row == target + u, 1.0, 0.0).astype(BF)
        spread = matmul(stacked, onehot)
        spread = spread[:count] + spread[count : 2 * count] + spread[2 * count :]
        spread = jnp.where(crossing, MASKED, spread)
        out[0, pl.ds(u, count, stride=WL), :] = spread[:, :128]
        out[1, pl.ds(u, count, stride=WL), :] = spread[:, 128:]


def main_kernel(
    parts, tok, dy, east, south, corner, bias, order, *refs
):
    dense = refs[:parts]
    send, keep, gain_sum, scores_grad, grad_qkv, unit_out, scale_out, qkv_w, proj_w, sums = refs[parts:]
    n_qkv, n_proj = 3 * C // parts, C // parts
    gain = None
    for k in range(parts):
        at = lax.rem(dp_index() + k, parts)
        qkv_w[pl.ds(pl.multiple_of(at * n_qkv, 16), n_qkv), :] = dense[k][:n_qkv]
        proj_w[pl.ds(pl.multiple_of(at * n_proj, 16), n_proj), :] = dense[k][n_qkv : n_qkv + n_proj]
        term = dense[k][n_qkv + n_proj : n_qkv + n_proj + 16].astype(F32)[:1]
        gain = term if gain is None else gain + term

    def own(ref):
        part = ref[:, SA:].astype(F32)
        return part[:, :, 4:12].reshape(QUAD, C).astype(BF)

    def window(ref, index):
        at = slice(index * QUAD, (index + 1) * QUAD)
        return jnp.concatenate([own(ref), east[at], south[at], corner[at]], axis=0)

    x = matmul(order[...], window(tok, 0))
    dyw = matmul(order[...], window(dy, 1)).astype(BF)
    average = jnp.sum(x, axis=-1, keepdims=True) * (1.0 / C)
    centred = x - average
    variance = jnp.sum(centred * centred, axis=-1, keepdims=True) * (1.0 / C)
    inverse = lax.rsqrt(variance + EPS)
    unit = centred * inverse
    normed = (unit * gain).astype(BF)
    qkv_t = matmul_t(qkv_w[...], normed).astype(BF)
    query = matmul_t(normed, qkv_w[:C]).astype(BF)
    grad_att32 = matmul(dyw, proj_w[...]).astype(BF).astype(F32)
    grad_att = grad_att32.astype(BF)
    grad_att_t = grad_att32.T.astype(BF)
    dy_t = dyw.astype(F32).T.astype(BF)
    scale = 1.0 / math.sqrt(HD)

    def alone(part, head):
        pieces = []
        if head:
            pieces.append(jnp.zeros((head * HD, WT), BF))
        pieces.append(part)
        if head < H - 1:
            pieces.append(jnp.zeros(((H - 1 - head) * HD, WT), BF))
        return jnp.concatenate(pieces, axis=0)

    def both(ref, at):
        rows = slice(at, at + WT)
        return jnp.concatenate([ref[0, rows], ref[1, rows, : WT - 128]], axis=1)

    attended_t, grad_q, grad_k, grad_v = [], [], [], []
    for head in range(H):
        at = head * HD
        q_t = qkv_t[at : at + HD]
        k_t = qkv_t[C + at : C + at + HD]
        v_t = qkv_t[2 * C + at : 2 * C + at + HD]
        scores = matmul(query, alone(k_t, head)) * scale + both(bias, head * WT)
        expo = jnp.exp(scores - jnp.max(scores, axis=-1, keepdims=True))
        probs = expo * (1.0 / jnp.sum(expo, axis=-1, keepdims=True))
        probs_low = probs.astype(BF)
        attended_t.append(matmul_t(v_t, probs_low))
        grad_probs = matmul(grad_att, alone(v_t, head))
        grad_v.append(matmul(grad_att_t[at : at + HD], probs_low))
        mean = jnp.sum(probs * grad_probs, axis=-1, keepdims=True)
        grad_scores = probs * (grad_probs - mean)
        scores_grad[0, head * WT : (head + 1) * WT] = grad_scores[:, :128]
        scores_grad[1, head * WT : (head + 1) * WT, : WT - 128] = grad_scores[:, 128:]
        scores_low = grad_scores.astype(BF)
        grad_q.append(matmul_t(k_t, scores_low) * scale)
        grad_k.append(matmul(q_t, scores_low) * scale)
    grad_qkv_t32 = jnp.concatenate(grad_q + grad_k + grad_v, axis=0)
    grad_qkv_t = grad_qkv_t32.astype(BF)
    grad_qkv_w = matmul(grad_qkv_t, normed)
    grad_proj = matmul_t(dy_t, jnp.concatenate(attended_t, axis=0).astype(BF))
    each = n_qkv + n_proj
    for k in range(parts):
        sums[k * each : k * each + n_qkv] = grad_qkv_w[k * n_qkv : (k + 1) * n_qkv]
        sums[k * each + n_qkv : (k + 1) * each] = grad_proj[k * n_proj : (k + 1) * n_proj]
    half = each // 2
    for k in range(parts):
        mine = k * each + side_index() * half
        other = k * each + (1 - side_index()) * half
        rows = slice(k * 3 * half // 4, (k + 1) * 3 * half // 4)
        keep[rows] = folded(sums[pl.ds(pl.multiple_of(mine, 16), half), :])
        send[rows] = folded(sums[pl.ds(pl.multiple_of(other, 16), half), :]).astype(BF)
    weighted = jnp.sum(grad_qkv_w * qkv_w[...].astype(F32), axis=0, keepdims=True)
    gain_sum[...] = jnp.broadcast_to(weighted / gain, (16, C))
    grad_qkv[...] = grad_qkv_t32
    unit_out[...] = unit
    scale_out[:WT] = jnp.broadcast_to(inverse, (WT, C))
    scale_out[WT:] = jnp.broadcast_to(gain, (16, C))


def table_kernel(scores_grad, table):
    count = H * ROWS
    row, target = offsets(288, WT, 0)
    total = jnp.zeros((count, 288), F32)
    for u in range(WL):
        onehot = jnp.where(row == target + u, 1.0, 0.0).astype(BF)
        rows = pl.ds(u, count, stride=WL)
        wide = jnp.concatenate(
            [scores_grad[0, rows, :], scores_grad[1, rows, :][:, : WT - 128]], axis=1
        )
        total += matmul_t(wide.astype(BF), onehot)
    tail = total[:, LEAD : LEAD + SPAN]
    tail = jnp.concatenate([tail[h * ROWS : (h + 1) * ROWS] for h in range(H)], axis=1)
    tail = jnp.concatenate([tail, jnp.zeros((ROWS, WIDE - H * SPAN), F32)], axis=1)
    table[:count] = total[:, :WIDE]
    table[count:] = jnp.concatenate([tail, jnp.zeros((16 - ROWS, WIDE), F32)], axis=0)


def token_kernel(grad_qkv_t, unit, scales, qkv_w, order_t, quads):
    grad_normed = matmul(grad_qkv_t[...].T.astype(BF), qkv_w[...])
    inverse = scales[:WT]
    scaled = grad_normed * scales[WT : WT + 1]
    first = jnp.sum(scaled, axis=-1, keepdims=True) * (1.0 / C)
    second = jnp.sum(scaled * unit[...], axis=-1, keepdims=True) * (1.0 / C)
    grad_x = inverse * (scaled - first - unit[...] * second)
    quads[...] = matmul(order_t[...], grad_x.astype(BF)).astype(BF)


def widened(rows):
    return jnp.concatenate([rows, jnp.zeros((rows.shape[0], WIDE - C), F32)], axis=1)


def dp_kernel(keep, got, gain_sum, table, mine, out):
    rows = keep.shape[0] // 2
    first = pl.ds(pl.multiple_of(dp_index() * rows, 16), rows)
    second = pl.ds(pl.multiple_of((1 - dp_index()) * rows, 16), rows)
    mine[...] = keep[first, :] + got[first, :].astype(F32)
    theirs = keep[second, :] + got[second, :].astype(F32)
    out[...] = jnp.concatenate([theirs, widened(gain_sum[...]), table[...]], axis=0).astype(BF)


def lat_kernel(mine, sent, got, quads, out, table):
    rows = mine.shape[0]
    sent, got = sent[...].astype(F32), got[...].astype(F32)
    dense = mine[...] + got[:rows]
    gain_sum = sent[rows : rows + 16] + got[rows : rows + 16]
    table[...] = (sent[rows + 16 :] + got[rows + 16 :]).astype(BF)
    halo = folded(quads[2 * QUAD :].astype(F32))
    out[...] = jnp.concatenate([dense, gain_sum, halo], axis=0).astype(BF)


def lat_next_kernel(sent, got, out):
    sent, got = sent[...].astype(F32), got[...].astype(F32)
    rows = sent.shape[0] - HALO
    out[...] = jnp.concatenate([sent[:rows] + got[:rows], sent[rows:]], axis=0).astype(BF)


def lon_kernel(sent, got, before, quads, table, out, south):
    sent, got, before = sent[...].astype(F32), got[...].astype(F32), before[...].astype(F32)
    rows = sent.shape[0] - HALO
    halo = jnp.where(lax.rem(lax.axis_index("lat"), 2) == 1, before[rows:], got[rows:])
    halo = unfolded(halo)
    south[...] = halo[:QUAD].astype(BF)
    east = jnp.concatenate([quads[QUAD : 2 * QUAD].astype(F32), halo[QUAD:]], axis=0)
    out[...] = jnp.concatenate(
        [sent[:rows] + got[:rows], folded(east), table[...].astype(F32)], axis=0
    ).astype(BF)


def lon_next_kernel(sent, got, out):
    sent, got = sent[...].astype(F32), got[...].astype(F32)
    rows = sent.shape[0] - HALO - TABLE
    out[...] = jnp.concatenate(
        [sent[:rows] + got[:rows], sent[rows : rows + HALO], sent[rows + HALO :] + got[rows + HALO :]],
        axis=0,
    ).astype(BF)


def last_kernel(
    dy, quads, south, before, sent, got, tokens_out, qkv_out, proj_out, gain_out, table_out,
    dense_s, gain_s, table_s, sems,
):
    sent, got, before = sent[...].astype(F32), got[...].astype(F32), before[...].astype(F32)
    rows = sent.shape[0] - HALO - TABLE - 16
    half = 4 * rows // 3
    dense_s[pl.ds(pl.multiple_of(side_index() * half, 16), half), :] = unfolded(sent[:rows])
    dense_s[pl.ds(pl.multiple_of((1 - side_index()) * half, 16), half), :] = unfolded(got[:rows])
    n_qkv = 3 * half // 2
    copies = [
        pltpu.make_async_copy(dense_s.at[:n_qkv], qkv_out, sems.at[0]),
        pltpu.make_async_copy(dense_s.at[n_qkv:], proj_out, sems.at[1]),
    ]
    for copy in copies:
        copy.start()
    at = rows + 16
    halo = jnp.where(lax.rem(lax.axis_index("lon"), 2) == 1, got[at : at + HALO], before[at : at + HALO])
    finish_tokens(dy, quads, south[...].astype(F32), unfolded(halo), tokens_out)
    table = sent[at + HALO :] + got[at + HALO :]
    count = H * ROWS
    tail = table[count : count + ROWS]
    tail = jnp.concatenate([tail[:, h * SPAN : (h + 1) * SPAN] for h in range(H)], axis=0)
    table = jnp.concatenate([table[:count, :LEAD], tail], axis=1)
    for h in range(H):
        pieces = [table[h * ROWS + a : h * ROWS + a + 1] for a in range(ROWS)]
        table_s[h] = jnp.concatenate(pieces, axis=1)
    copies.append(pltpu.make_async_copy(table_s, table_out, sems.at[2]))
    copies[-1].start()
    gain_sum = sent[rows : rows + 1] + got[rows : rows + 1]
    gain_s[...] = jnp.where(dp_index() == 0, gain_sum[:, : C // 2], gain_sum[:, C // 2 : C])
    copies.append(pltpu.make_async_copy(gain_s, gain_out, sems.at[3]))
    copies[-1].start()
    for copy in copies:
        copy.wait()


def finish_tokens(dy, quad, south, lon_halo, out):
    gap = jnp.zeros((WZ, SA, 4, C), F32)

    def low(value):
        return jnp.concatenate([value.reshape(WZ, SA, 8, C), gap], axis=2)

    def high(value):
        return jnp.concatenate([gap, value.reshape(WZ, SA, 8, C)], axis=2)

    upper = dy[:, :SA].astype(F32) + low(lon_halo[QUAD:]) + high(south)
    lower = dy[:, SA:].astype(F32) + low(lon_halo[:QUAD]) + high(quad[:QUAD].astype(F32))
    out[:, :SA] = upper.astype(BF)
    out[:, SA:] = lower.astype(BF)


def finish_kernel(dy, quad, south, lon_halo, out):
    finish_tokens(dy, quad, south[...].astype(F32), lon_halo[...].astype(F32), out)


def call(kernel, outs, scratch=(), specs=None, flops=1000000, nbytes=1000000, out_specs=None):
    return pl.pallas_call(
        kernel,
        out_shape=outs,
        in_specs=specs,
        out_specs=jax.tree.map(lambda _: VMEM, outs) if out_specs is None else out_specs,
        scratch_shapes=list(scratch),
        compiler_params=pltpu.CompilerParams(vmem_limit_bytes=24 << 20),
        cost_estimate=pl.CostEstimate(flops=flops, bytes_accessed=nbytes, transcendentals=0),
    )


def shaped(rows, cols, dtype):
    return jax.ShapeDtypeStruct((rows, cols), dtype)


def exchanged(value, axis, flip):
    count = lax.axis_size(axis)
    return lax.ppermute(value, axis, [(i, i ^ flip) for i in range(count)])


def passed_along(value, axis, steps):
    count = lax.axis_size(axis)
    return lax.ppermute(value, axis, [(i, (i + steps) % count) for i in range(count)])


def passed_diagonally(value, steps):
    rows, cols = lax.axis_size("lon"), lax.axis_size("lat")
    pairs = [
        (i * cols + j, ((i + steps) % rows) * cols + (j + steps) % cols)
        for i in range(rows)
        for j in range(cols)
    ]
    return lax.ppermute(value, ("lon", "lat"), pairs)


def body(tokens, grad_out, qkv_weight, proj_weight, norm_gain, bias_table):
    parts = lax.axis_size("dp")
    lon_count, lat_count = lax.axis_size("lon"), lax.axis_size("lat")
    n_qkv, n_proj = 3 * C // parts, C // parts
    each = n_qkv + n_proj
    half = each // 2
    tok = tokens.reshape(WZ, WA, WL, C)
    dy = grad_out.reshape(WZ, WA, WL, C)

    strips = [shaped(2 * QUAD, C, BF)] * 3
    dense, east, south, corner = call(
        functools.partial(pack_kernel, parts),
        [shaped(each + 16, C, BF)] + strips,
        specs=[VMEM] * 5,
    )(tok, dy, qkv_weight, proj_weight, norm_gain.reshape(1, n_proj))
    gathered = [dense] + [passed_along(dense, "dp", -k) for k in range(1, parts)]
    east = passed_along(east, "lon", -1)
    south = passed_along(south, "lat", -1)
    corner = passed_diagonally(corner, -1)
    bias = call(
        bias_kernel,
        jax.ShapeDtypeStruct((2, H * WT, 128), F32),
        specs=[VMEM],
        flops=200000000,
    )(bias_table.reshape(H * ROWS, ROWS * SPAN))
    order = token_order()
    packed = parts * 3 * half // 4
    outs = [
        shaped(packed, WIDE, BF),
        shaped(packed, WIDE, F32),
        shaped(16, C, F32),
        jax.ShapeDtypeStruct((2, H * WT, 128), F32),
        shaped(3 * C, WT, F32),
        shaped(WT, C, F32),
        shaped(WT + 16, C, F32),
        shaped(3 * C, C, BF),
    ]
    scratch = [pltpu.VMEM((C, C), BF), pltpu.VMEM((4 * C, C), F32)]
    send, keep, gain_sum, scores_grad, grad_qkv, unit, scales, qkv_full = call(
        functools.partial(main_kernel, parts), outs, scratch, specs=[VMEM] * (7 + parts)
    )(tok, dy, east, south, corner, bias, jnp.asarray(order, BF), *gathered)
    fast = (lon_count, lat_count, parts) == (4, 4, 2)
    if fast:
        got = exchanged(send, "lon", 1)
    table = call(table_kernel, shaped(TABLE, WIDE, F32), specs=[VMEM], flops=200000000)(scores_grad)
    if fast:
        mine, sent = call(
            dp_kernel,
            [shaped(packed // 2, WIDE, F32), shaped(packed // 2 + 16 + TABLE, WIDE, BF)],
            specs=[VMEM] * 4,
        )(keep, got, gain_sum, table)
        got = exchanged(sent, "dp", 1)
    quads = call(token_kernel, shaped(4 * QUAD, C, BF), specs=[VMEM] * 5, flops=100000000)(
        grad_qkv, unit, scales, qkv_full, jnp.asarray(order.T, BF)
    )
    if fast:
        rows = packed // 2 + 16
        lat_shape = shaped(rows + HALO, WIDE, BF)
        sent, table = call(
            lat_kernel, [lat_shape, shaped(TABLE, WIDE, BF)], specs=[VMEM] * 4
        )(mine, sent, got, quads)
        before = exchanged(sent, "lat", 1)
        sent = call(lat_next_kernel, lat_shape, specs=[VMEM] * 2)(sent, before)
        got = exchanged(sent, "lat", 3)
        lon_shape = shaped(rows + HALO + TABLE, WIDE, BF)
        sent, south = call(
            lon_kernel, [lon_shape, shaped(QUAD, C, BF)], specs=[VMEM] * 5
        )(sent, got, before, quads, table)
        before = exchanged(sent, "lon", 3)
        sent = call(lon_next_kernel, lon_shape, specs=[VMEM] * 2)(sent, before)
        got = exchanged(sent, "lon", 1)
        tile = (WZ, WA, WL, C)
        grad_tokens, grad_qkv_w, grad_proj, grad_gain, grad_table = call(
            last_kernel,
            [
                jax.ShapeDtypeStruct(tile, BF),
                shaped(n_qkv, C, F32),
                shaped(n_proj, C, F32),
                shaped(1, n_proj, F32),
                jax.ShapeDtypeStruct((H, 1, POS), F32),
            ],
            [
                pltpu.VMEM((each, C), F32),
                pltpu.VMEM((1, n_proj), F32),
                pltpu.VMEM((H, 1, POS), F32),
                pltpu.SemaphoreType.DMA((4,)),
            ],
            specs=[VMEM] * 6,
            out_specs=[VMEM] + [pl.BlockSpec(memory_space=pltpu.HBM)] * 4,
        )(dy, quads, south, before, sent, got)
        return (
            grad_tokens.reshape(tokens.shape),
            grad_qkv_w,
            grad_proj,
            grad_gain.reshape(n_proj),
            grad_table.reshape(1, H, POS),
        )
    pair = jnp.stack([keep, send.astype(F32)]).reshape(2, parts, packed // parts, WIDE)
    pair = jnp.where(side_index() == 0, pair, pair[::-1])
    pair = jax.vmap(jax.vmap(unfolded))(pair)
    dense_sum = lax.psum(pair.transpose(1, 0, 2, 3).reshape(parts * each, C), ("lon", "lat"))
    total = lax.psum_scatter(dense_sum, "dp", scatter_dimension=0, tiled=True)
    grad_gain = lax.psum(gain_sum[0], ("lon", "lat"))
    grad_gain = lax.psum_scatter(grad_gain, "dp", scatter_dimension=0, tiled=True)
    table = lax.psum(table, ("lon", "dp"))
    count = H * ROWS
    tail = table[count : count + ROWS, : H * SPAN].reshape(ROWS, H, SPAN)
    tail = tail.transpose(1, 0, 2).reshape(count, SPAN)
    table = jnp.concatenate([table[:count, :LEAD], tail], axis=1)
    south_halo = passed_along(quads[2 * QUAD :], "lat", 1)
    east_halo = jnp.concatenate([quads[QUAD : 2 * QUAD], south_halo[QUAD:]])
    east_halo = passed_along(east_halo, "lon", 1)
    grad_tokens = call(
        finish_kernel, jax.ShapeDtypeStruct((WZ, WA, WL, C), BF), specs=[VMEM] * 4
    )(dy, quads, south_halo[:QUAD], east_halo)
    return (
        grad_tokens.reshape(tokens.shape),
        total[:n_qkv],
        total[n_qkv:],
        grad_gain,
        table.reshape(1, H, POS),
    )


def solution(mesh):
    spec = P("dp", None, "lat", "lon", None)
    return jax.shard_map(
        body,
        mesh=mesh,
        in_specs=(spec, spec, P("dp", None), P("dp", None), P("dp"), P("lat", None, None)),
        out_specs=(spec, P("dp", None), P("dp", None), P("dp"), P("lat", None, None)),
        check_vma=False,
    )
```

```python
import functools
import math

import jax
import jax.numpy as jnp
import numpy as np
from jax import lax
from jax.experimental import pallas as pl
from jax.experimental.pallas import tpu as pltpu
from jax.sharding import PartitionSpec as P

C = 192
H = 6
HD = 32
WZ = 2
WA = 6
WL = 12
SA = 3
SO = 6
WT = 144
POS = 3312
EPS = 1e-05
MASKED = -1e30

ROWS = WZ * WA
SPAN = 2 * WL - 1
QUAD = WZ * SA * 8
WIDE = 256
LEAD = 11 * SPAN
HALO = 3 * QUAD // 2
TABLE = H * ROWS + 16
BF = jnp.bfloat16
F32 = jnp.float32
VMEM = pl.BlockSpec(memory_space=pltpu.VMEM)


def dp_index():
    return lax.axis_index("dp")


def side_index():
    column = lax.axis_index("lon")
    return lax.rem(column + lax.div(column, 2), 2)


def last_row():
    return lax.axis_index("lat") == lax.axis_size("lat") - 1


def token_order():
    order = np.zeros((WT, 4 * QUAD), np.float32)
    for z in range(WZ):
        for a in range(WA):
            for o in range(WL):
                south, east = a >= SA, o >= SO
                quadrant = 2 * south + east
                column = o - SO if east else o + 2
                row = (z * SA + a % SA) * 8 + column
                order[(z * WA + a) * WL + o, quadrant * QUAD + row] = 1.0
    return order


def matmul(a, b):
    return lax.dot_general(a, b, (((1,), (0,)), ((), ())), preferred_element_type=F32)


def matmul_t(a, b):
    return lax.dot_general(a, b, (((1,), (1,)), ((), ())), preferred_element_type=F32)


def over_12(index):
    return lax.shift_right_logical(index * 5462, 16)


def spread_lanes(row, position, parts):
    width = row.shape[1]
    full = jnp.zeros((1, C), F32)
    for k in range(parts):
        pieces = [row]
        if k:
            pieces.insert(0, jnp.zeros((1, k * width), F32))
        if k < parts - 1:
            pieces.append(jnp.zeros((1, (parts - 1 - k) * width), F32))
        full = jnp.where(position == k, jnp.concatenate(pieces, axis=1), full)
    return full


def folded(value):
    rows = value.shape[0]
    top, tail = value[: 3 * rows // 4], value[3 * rows // 4 :]
    side = jnp.concatenate([tail[:, at : at + 64] for at in (0, 64, 128)], axis=0)
    return jnp.concatenate([top, side], axis=1)


def unfolded(value):
    rows = value.shape[0] // 3
    side = value[:, C:]
    tail = jnp.concatenate([side[k * rows : (k + 1) * rows] for k in range(3)], axis=1)
    return jnp.concatenate([value[:, :C], tail], axis=0)


def pack_kernel(parts, tok, dy, qkv, proj, gain, dense, east, south, corner):
    n_qkv, n_proj = 3 * C // parts, C // parts
    dense[:n_qkv] = qkv[...]
    dense[n_qkv : n_qkv + n_proj] = proj[...]
    row = spread_lanes(gain[...].astype(F32), dp_index(), parts)
    dense[n_qkv + n_proj :] = jnp.broadcast_to(row, (16, C)).astype(BF)

    def strips(rows, cols):
        pair = []
        for ref in (tok, dy):
            part = ref[:, rows : rows + SA].astype(F32)
            pair.append(part[:, :, cols : cols + 8].reshape(QUAD, C))
        return folded(jnp.concatenate(pair, axis=0)).astype(BF)

    east[...] = strips(SA, 0)
    south[...] = strips(0, 4)
    corner[...] = strips(0, 0)


def offsets(height, width, half):
    row = lax.broadcasted_iota(jnp.int32, (height, width), 0)
    col = lax.broadcasted_iota(jnp.int32, (height, width), 1)
    block = over_12(col)
    return row, block * SPAN - (col - block * WL) + WL - 1 - half


def bias_kernel(table, out):
    values = table[...]
    high = values.astype(BF)
    rest = values - high.astype(F32)
    middle = rest.astype(BF)
    low = (rest - middle.astype(F32)).astype(BF)
    stacked = jnp.concatenate([high, middle, low], axis=0)
    row, target = offsets(ROWS * SPAN, WIDE, 0)
    count = H * ROWS
    here = lax.broadcasted_iota(jnp.int32, (count, WIDE), 0)
    here = here - over_12(here) * ROWS
    there = over_12(lax.broadcasted_iota(jnp.int32, (count, WIDE), 1))

    def wrapped(index):
        return jnp.where(index >= WA, index - WA, index) >= SA

    crossing = jnp.logical_and(wrapped(here) != wrapped(there), last_row())
    for u in range(WL):
        onehot = jnp.where(row == target + u, 1.0, 0.0).astype(BF)
        spread = matmul(stacked, onehot)
        spread = spread[:count] + spread[count : 2 * count] + spread[2 * count :]
        spread = jnp.where(crossing, MASKED, spread)
        out[0, pl.ds(u, count, stride=WL), :] = spread[:, :128]
        out[1, pl.ds(u, count, stride=WL), :] = spread[:, 128:]


def main_kernel(
    parts, pieces, south, corner, east, tok, dy, bias, order, *refs
):
    dense = refs[:parts]
    send, keep, gain_sum, scores_grad, grad_qkv, unit_out, scale_out, qkv_w, proj_w, sums = refs[parts:]
    n_qkv, n_proj = 3 * C // parts, C // parts
    gain = None
    for k in range(parts):
        at = lax.rem(dp_index() + k, parts)
        qkv_w[pl.ds(pl.multiple_of(at * n_qkv, 16), n_qkv), :] = dense[k][:n_qkv]
        proj_w[pl.ds(pl.multiple_of(at * n_proj, 16), n_proj), :] = dense[k][n_qkv : n_qkv + n_proj]
        term = dense[k][n_qkv + n_proj : n_qkv + n_proj + 16].astype(F32)[:1]
        gain = term if gain is None else gain + term

    def own(ref):
        part = ref[:, SA:].astype(F32)
        return part[:, :, 4:12].reshape(QUAD, C).astype(BF)

    halos = [unfolded(ref[...].astype(F32)).astype(BF) for ref in (east, south, corner)]

    def window(ref, index):
        at = slice(index * QUAD, (index + 1) * QUAD)
        return jnp.concatenate([own(ref)] + [halo[at] for halo in halos], axis=0)

    x = matmul(order[...], window(tok, 0))
    dyw = matmul(order[...], window(dy, 1)).astype(BF)
    average = jnp.sum(x, axis=-1, keepdims=True) * (1.0 / C)
    centred = x - average
    variance = jnp.sum(centred * centred, axis=-1, keepdims=True) * (1.0 / C)
    inverse = lax.rsqrt(variance + EPS)
    unit = centred * inverse
    normed = (unit * gain).astype(BF)
    qkv_t = matmul_t(qkv_w[...], normed).astype(BF)
    query = matmul_t(normed, qkv_w[:C]).astype(BF)
    grad_att32 = matmul(dyw, proj_w[...]).astype(BF).astype(F32)
    grad_att = grad_att32.astype(BF)
    grad_att_t = grad_att32.T.astype(BF)
    dy_t = dyw.astype(F32).T.astype(BF)
    scale = 1.0 / math.sqrt(HD)

    def alone(part, head):
        pieces = []
        if head:
            pieces.append(jnp.zeros((head * HD, WT), BF))
        pieces.append(part)
        if head < H - 1:
            pieces.append(jnp.zeros(((H - 1 - head) * HD, WT), BF))
        return jnp.concatenate(pieces, axis=0)

    def both(ref, at):
        rows = slice(at, at + WT)
        return jnp.concatenate([ref[0, rows], ref[1, rows, : WT - 128]], axis=1)

    attended_t, grad_q, grad_k, grad_v = [], [], [], []
    for head in range(H):
        at = head * HD
        q_t = qkv_t[at : at + HD]
        k_t = qkv_t[C + at : C + at + HD]
        v_t = qkv_t[2 * C + at : 2 * C + at + HD]
        scores = matmul(query, alone(k_t, head)) * scale + both(bias, head * WT)
        expo = jnp.exp(scores - jnp.max(scores, axis=-1, keepdims=True))
        probs = expo * (1.0 / jnp.sum(expo, axis=-1, keepdims=True))
        probs_low = probs.astype(BF)
        attended_t.append(matmul_t(v_t, probs_low))
        grad_probs = matmul(grad_att, alone(v_t, head))
        grad_v.append(matmul(grad_att_t[at : at + HD], probs_low))
        mean = jnp.sum(probs * grad_probs, axis=-1, keepdims=True)
        grad_scores = probs * (grad_probs - mean)
        scores_grad[0, head * WT : (head + 1) * WT] = grad_scores[:, :128]
        scores_grad[1, head * WT : (head + 1) * WT, : WT - 128] = grad_scores[:, 128:]
        scores_low = grad_scores.astype(BF)
        grad_q.append(matmul_t(k_t, scores_low) * scale)
        grad_k.append(matmul(q_t, scores_low) * scale)
    grad_qkv_t32 = jnp.concatenate(grad_q + grad_k + grad_v, axis=0)
    grad_qkv_t = grad_qkv_t32.astype(BF)
    grad_qkv_w = matmul(grad_qkv_t, normed)
    grad_proj = matmul_t(dy_t, jnp.concatenate(attended_t, axis=0).astype(BF))
    each = n_qkv + n_proj
    for k in range(parts):
        sums[k * each : k * each + n_qkv] = grad_qkv_w[k * n_qkv : (k + 1) * n_qkv]
        sums[k * each + n_qkv : (k + 1) * each] = grad_proj[k * n_proj : (k + 1) * n_proj]
    half = each // 2
    size = half // pieces
    for k in range(parts):
        for p in range(pieces):
            mine = k * each + side_index() * half + p * size
            other = k * each + (1 - side_index()) * half + p * size
            at = (k * pieces + p) * 3 * size // 4
            rows = slice(at, at + 3 * size // 4)
            keep[rows] = folded(sums[pl.ds(pl.multiple_of(mine, 16), size), :])
            send[rows] = folded(sums[pl.ds(pl.multiple_of(other, 16), size), :]).astype(BF)
    weighted = jnp.sum(grad_qkv_w * qkv_w[...].astype(F32), axis=0, keepdims=True)
    gain_sum[...] = jnp.broadcast_to(weighted / gain, (8, C))
    grad_qkv[...] = grad_qkv_t32
    unit_out[...] = unit
    scale_out[:WT] = jnp.broadcast_to(inverse, (WT, C))
    scale_out[WT:] = jnp.broadcast_to(gain, (16, C))


def table_kernel(scores_grad, table):
    count = H * ROWS
    row, target = offsets(288, WT, 0)
    total = jnp.zeros((count, 288), F32)
    for u in range(WL):
        onehot = jnp.where(row == target + u, 1.0, 0.0).astype(BF)
        rows = pl.ds(u, count, stride=WL)
        wide = jnp.concatenate(
            [scores_grad[0, rows, :], scores_grad[1, rows, :][:, : WT - 128]], axis=1
        )
        total += matmul_t(wide.astype(BF), onehot)
    tail = total[:, LEAD : LEAD + SPAN]
    tail = jnp.concatenate([tail[h * ROWS : (h + 1) * ROWS] for h in range(H)], axis=1)
    tail = jnp.concatenate([tail, jnp.zeros((ROWS, WIDE - H * SPAN), F32)], axis=1)
    rest = jnp.zeros((16 - ROWS, WIDE), F32)
    table[...] = jnp.concatenate([total[:, :WIDE], tail, rest], axis=0).astype(BF)


def token_kernel(grad_qkv_t, unit, scales, qkv_w, order_t, quads, south):
    grad_normed = matmul(grad_qkv_t[...].T.astype(BF), qkv_w[...])
    inverse = scales[:WT]
    scaled = grad_normed * scales[WT : WT + 1]
    first = jnp.sum(scaled, axis=-1, keepdims=True) * (1.0 / C)
    second = jnp.sum(scaled * unit[...], axis=-1, keepdims=True) * (1.0 / C)
    grad_x = inverse * (scaled - first - unit[...] * second)
    every = matmul(order_t[...], grad_x.astype(BF))
    quads[...] = every[: 2 * QUAD].astype(BF)
    south[...] = folded(every[2 * QUAD :]).astype(BF)


def east_kernel(quads, south, east):
    corner = unfolded(south[...].astype(F32))[QUAD:]
    east[...] = folded(jnp.concatenate([quads[QUAD:].astype(F32), corner], axis=0)).astype(BF)


def finish_kernel(dy, quads, south, east, out):
    gap = jnp.zeros((WZ, SA, 4, C), F32)

    def low(value):
        return jnp.concatenate([value.reshape(WZ, SA, 8, C), gap], axis=2)

    def high(value):
        return jnp.concatenate([gap, value.reshape(WZ, SA, 8, C)], axis=2)

    lon_halo = unfolded(east[...].astype(F32))
    lat_halo = unfolded(south[...].astype(F32))[:QUAD]
    upper = dy[:, :SA].astype(F32) + low(lon_halo[QUAD:]) + high(lat_halo)
    lower = dy[:, SA:].astype(F32) + low(lon_halo[:QUAD]) + high(quads[:QUAD].astype(F32))
    out[:, :SA] = upper.astype(BF)
    out[:, SA:] = lower.astype(BF)


def widened(rows):
    return jnp.concatenate([rows, jnp.zeros((rows.shape[0], WIDE - C), F32)], axis=1)


def chip_index():
    return lax.div(lax.axis_index("lon"), 2)


def plane_kernel(keep, got, gain_sum, table, mine, to_dp, to_lon, to_both):
    rows = keep.shape[0] // 4

    def piece(other_dp, other_chip):
        dp = dp_index() if not other_dp else 1 - dp_index()
        chip = chip_index() if not other_chip else 1 - chip_index()
        at = pl.ds(pl.multiple_of((2 * dp + chip) * rows, 8), rows)
        return keep[at, :] + got[at, :].astype(F32)

    mine[...] = piece(False, False)
    to_dp[...] = jnp.concatenate(
        [piece(True, False), widened(gain_sum[...]), table[...].astype(F32)], axis=0
    ).astype(BF)
    to_lon[...] = piece(False, True).astype(BF)
    to_both[...] = piece(True, True).astype(BF)


def plane_sum_kernel(mine, sent, from_both, from_dp, from_lon, halo, out, table):
    rows = mine.shape[0]
    got = from_dp[...].astype(F32)
    dense = mine[...] + got[:rows] + from_lon[...].astype(F32) + from_both[...].astype(F32)
    shared = sent[...].astype(F32)[rows:] + got[rows:]
    out[...] = jnp.concatenate([dense, shared[:8], halo[...].astype(F32)], axis=0).astype(BF)
    table[...] = shared[8:].astype(BF)


def sum_kernel(sent, got, out):
    out[...] = (sent[...].astype(F32) + got[...].astype(F32)).astype(BF)


def relay_kernel(sent, got, out):
    sent, got = sent[...].astype(F32), got[...].astype(F32)
    rows = sent.shape[0] - HALO
    out[...] = jnp.concatenate([sent[:rows] + got[:rows], sent[rows:]], axis=0).astype(BF)


def lon_kernel(sent, got, before, quads, out, south, east):
    sent, got = sent[...].astype(F32), got[...].astype(F32)
    rows = sent.shape[0] - HALO
    halo = jnp.where(
        lax.rem(lax.axis_index("lat"), 2) == 1, before[...].astype(F32)[rows:], got[rows:]
    )
    south[...] = halo.astype(BF)
    corner = unfolded(halo)[QUAD:]
    halo = folded(jnp.concatenate([quads[QUAD:].astype(F32), corner], axis=0))
    east[...] = halo.astype(BF)
    out[...] = jnp.concatenate([sent[:rows] + got[:rows], halo], axis=0).astype(BF)


def join_kernel(sent, got, out):
    sent, got = sent[...].astype(F32), got[...].astype(F32)
    rows = sent.shape[0] - HALO - 8
    first = chip_index() == 0
    low = jnp.where(first, sent[:rows], got[:rows])
    high = jnp.where(first, got[:rows], sent[:rows])
    gain_sum = sent[rows : rows + 8] + got[rows : rows + 8]
    out[...] = jnp.concatenate([low, high, gain_sum], axis=0).astype(BF)


def choose_kernel(got, earlier, out):
    rows = earlier.shape[0] - HALO
    earlier = earlier[...].astype(F32)[rows:]
    odd = lax.rem(lax.axis_index("lon"), 2) == 1
    out[...] = jnp.where(odd, got[...].astype(F32), earlier).astype(BF)


def last_table_kernel(sent, got, table_out, table_s, sem):
    table = sent[...].astype(F32) + got[...].astype(F32)
    count = H * ROWS
    tail = table[count : count + ROWS]
    tail = jnp.concatenate([tail[:, h * SPAN : (h + 1) * SPAN] for h in range(H)], axis=0)
    table = jnp.concatenate([table[:count, :LEAD], tail], axis=1)
    for h in range(H):
        rows = [table[h * ROWS + a : h * ROWS + a + 1] for a in range(ROWS)]
        table_s[h] = jnp.concatenate(rows, axis=1)
    copy = pltpu.make_async_copy(table_s, table_out, sem)
    copy.start()
    copy.wait()


def last_kernel(sent, got, qkv_out, proj_out, gain_out, dense_s, gain_s, sems):
    sent, got = sent[...].astype(F32), got[...].astype(F32)
    rows = (sent.shape[0] - 8) // 2
    size = 4 * rows // 3
    gain_sum = sent[2 * rows : 2 * rows + 1] + got[2 * rows : 2 * rows + 1]
    gain_s[...] = jnp.where(dp_index() == 0, gain_sum[:, : C // 2], gain_sum[:, C // 2 : C])
    for side, value in ((side_index(), sent), (1 - side_index(), got)):
        for p in range(2):
            at = pl.ds(pl.multiple_of((2 * side + p) * size, 16), size)
            dense_s[at, :] = unfolded(value[p * rows : (p + 1) * rows])
    copies = [
        pltpu.make_async_copy(dense_s.at[: 3 * size], qkv_out, sems.at[0]),
        pltpu.make_async_copy(dense_s.at[3 * size :], proj_out, sems.at[1]),
        pltpu.make_async_copy(gain_s, gain_out, sems.at[2]),
    ]
    for copy in copies:
        copy.start()
    for copy in copies:
        copy.wait()


def call(kernel, outs, scratch=(), specs=None, flops=1000000, nbytes=1000000, out_specs=None):
    return pl.pallas_call(
        kernel,
        out_shape=outs,
        in_specs=specs,
        out_specs=jax.tree.map(lambda _: VMEM, outs) if out_specs is None else out_specs,
        scratch_shapes=list(scratch),
        compiler_params=pltpu.CompilerParams(vmem_limit_bytes=24 << 20),
        cost_estimate=pl.CostEstimate(flops=flops, bytes_accessed=nbytes, transcendentals=0),
    )


def shaped(rows, cols, dtype):
    return jax.ShapeDtypeStruct((rows, cols), dtype)


def exchanged(value, axis, flip):
    count = lax.axis_size(axis)
    return lax.ppermute(value, axis, [(i, i ^ flip) for i in range(count)])


def exchanged_both(value):
    pairs = [(2 * i + k, 2 * (i ^ 3) + (1 - k)) for i in range(4) for k in range(2)]
    return lax.ppermute(value, ("lon", "dp"), pairs)


def tied(*values):
    return lax.optimization_barrier(values)


def passed_along(value, axis, steps):
    count = lax.axis_size(axis)
    return lax.ppermute(value, axis, [(i, (i + steps) % count) for i in range(count)])


def passed_diagonally(value, steps):
    rows, cols = lax.axis_size("lon"), lax.axis_size("lat")
    pairs = [
        (i * cols + j, ((i + steps) % rows) * cols + (j + steps) % cols)
        for i in range(rows)
        for j in range(cols)
    ]
    return lax.ppermute(value, ("lon", "lat"), pairs)


def body(tokens, grad_out, qkv_weight, proj_weight, norm_gain, bias_table):
    parts = lax.axis_size("dp")
    lon_count, lat_count = lax.axis_size("lon"), lax.axis_size("lat")
    fast = (lon_count, lat_count, parts) == (4, 4, 2)
    n_qkv, n_proj = 3 * C // parts, C // parts
    each = n_qkv + n_proj
    half = each // 2
    tok = tokens.reshape(WZ, WA, WL, C)
    dy = grad_out.reshape(WZ, WA, WL, C)

    strips = [shaped(HALO, WIDE, BF)] * 3
    dense, east, south, corner = call(
        functools.partial(pack_kernel, parts), [shaped(each + 16, C, BF)] + strips, specs=[VMEM] * 5
    )(tok, dy, qkv_weight, proj_weight, norm_gain.reshape(1, n_proj))
    gathered = [dense] + [passed_along(dense, "dp", -k) for k in range(1, parts)]
    south = passed_along(south, "lat", -1)
    corner = passed_diagonally(corner, -1)
    east = passed_along(east, "lon", -1)
    bias = call(
        bias_kernel,
        jax.ShapeDtypeStruct((2, H * WT, 128), F32),
        specs=[VMEM],
        flops=200000000,
    )(bias_table.reshape(H * ROWS, ROWS * SPAN))
    order = token_order()
    packed = parts * 3 * half // 4
    outs = [
        shaped(packed, WIDE, BF),
        shaped(packed, WIDE, F32),
        shaped(8, C, F32),
        jax.ShapeDtypeStruct((2, H * WT, 128), F32),
        shaped(3 * C, WT, F32),
        shaped(WT, C, F32),
        shaped(WT + 16, C, F32),
        shaped(3 * C, C, BF),
    ]
    scratch = [pltpu.VMEM((C, C), BF), pltpu.VMEM((4 * C, C), F32)]
    send, keep, gain_sum, scores_grad, grad_qkv, unit, scales, qkv_full = call(
        functools.partial(main_kernel, parts, 2 if fast else 1),
        outs,
        scratch,
        specs=[VMEM] * (7 + parts),
    )(south, corner, east, tok, dy, bias, jnp.asarray(order, BF), *gathered)
    if fast:
        got = exchanged(send, "lon", 1)
    table = call(table_kernel, shaped(TABLE, WIDE, BF), specs=[VMEM], flops=200000000)(scores_grad)
    if fast:
        piece = packed // 4
        mine, sent, to_lon, to_both = call(
            plane_kernel,
            [
                shaped(piece, WIDE, F32),
                shaped(piece + 8 + TABLE, WIDE, BF),
                shaped(piece, WIDE, BF),
                shaped(piece, WIDE, BF),
            ],
            specs=[VMEM] * 4,
        )(keep, got, gain_sum, table)
        from_both = exchanged_both(to_both)
        got = exchanged(sent, "dp", 1)
        from_lon = exchanged(to_lon, "lon", 3)
    quads, south = call(
        token_kernel,
        [shaped(2 * QUAD, C, BF), shaped(HALO, WIDE, BF)],
        specs=[VMEM] * 5,
        flops=100000000,
    )(grad_qkv, unit, scales, qkv_full, jnp.asarray(order.T, BF))
    if fast:
        lat_shape = shaped(piece + 8 + HALO, WIDE, BF)
        table_shape = shaped(TABLE, WIDE, BF)
        halo_shape = shaped(HALO, WIDE, BF)
        sent, table = call(plane_sum_kernel, [lat_shape, table_shape], specs=[VMEM] * 6)(
            mine, sent, from_both, got, from_lon, south
        )
        before = exchanged(sent, "lat", 1)
        sent = call(relay_kernel, lat_shape, specs=[VMEM] * 2)(sent, before)
        sent, table = tied(sent, table)
        got = exchanged(sent, "lat", 3)
        table_got = exchanged(table, "lon", 3)
        sent, south, east = call(
            lon_kernel, [lat_shape, halo_shape, halo_shape], specs=[VMEM] * 4
        )(sent, got, before, quads)
        sent, table_got = tied(sent, table_got)
        got = exchanged(sent, "lon", 3)
        table = call(sum_kernel, table_shape, specs=[VMEM] * 2)(table, table_got)
        table_got = exchanged(table, "lon", 1)
        east_got = exchanged(east, "lon", 1)
        east = call(choose_kernel, halo_shape, specs=[VMEM] * 2)(east_got, got)
    else:
        south = passed_along(south, "lat", 1)
        east = call(east_kernel, shaped(HALO, WIDE, BF), specs=[VMEM] * 2)(quads, south)
        east = passed_along(east, "lon", 1)
    tile = (WZ, WA, WL, C)
    finish = call(finish_kernel, jax.ShapeDtypeStruct(tile, BF), specs=[VMEM] * 4)
    hbm = pl.BlockSpec(memory_space=pltpu.HBM)
    if fast:
        sent = call(join_kernel, shaped(2 * piece + 8, WIDE, BF), specs=[VMEM] * 2)(sent, got)
        sent, table_got, east = tied(sent, table_got, east)
        got = exchanged(sent, "lon", 1)
        grad_table = call(
            last_table_kernel,
            jax.ShapeDtypeStruct((H, 1, POS), F32),
            [pltpu.VMEM((H, 1, POS), F32), pltpu.SemaphoreType.DMA],
            specs=[VMEM] * 2,
            out_specs=hbm,
        )(table, table_got).reshape(1, H, POS)
        grad_tokens = finish(dy, quads, south, east).reshape(tokens.shape)
        got, grad_tokens, grad_table = tied(got, grad_tokens, grad_table)
        grad_qkv_w, grad_proj, grad_gain = call(
            last_kernel,
            [shaped(n_qkv, C, F32), shaped(n_proj, C, F32), shaped(1, n_proj, F32)],
            [
                pltpu.VMEM((each, C), F32),
                pltpu.VMEM((1, n_proj), F32),
                pltpu.SemaphoreType.DMA((3,)),
            ],
            specs=[VMEM] * 2,
            out_specs=[hbm] * 3,
        )(sent, got)
        return grad_tokens, grad_qkv_w, grad_proj, grad_gain.reshape(n_proj), grad_table
    grad_tokens = finish(dy, quads, south, east).reshape(tokens.shape)
    pair = jnp.stack([keep, send.astype(F32)]).reshape(2, parts, packed // parts, WIDE)
    pair = jnp.where(side_index() == 0, pair, pair[::-1])
    pair = jax.vmap(jax.vmap(unfolded))(pair)
    dense_sum = lax.psum(pair.transpose(1, 0, 2, 3).reshape(parts * each, C), ("lon", "lat"))
    total = lax.psum_scatter(dense_sum, "dp", scatter_dimension=0, tiled=True)
    grad_gain = lax.psum(gain_sum[0], ("lon", "lat"))
    grad_gain = lax.psum_scatter(grad_gain, "dp", scatter_dimension=0, tiled=True)
    table = lax.psum(table.astype(F32), ("lon", "dp"))
    count = H * ROWS
    tail = table[count : count + ROWS, : H * SPAN].reshape(ROWS, H, SPAN)
    tail = tail.transpose(1, 0, 2).reshape(count, SPAN)
    table = jnp.concatenate([table[:count, :LEAD], tail], axis=1)
    return (
        grad_tokens,
        total[:n_qkv],
        total[n_qkv:],
        grad_gain,
        table.reshape(1, H, POS),
    )


def solution(mesh):
    spec = P("dp", None, "lat", "lon", None)
    return jax.shard_map(
        body,
        mesh=mesh,
        in_specs=(spec, spec, P("dp", None), P("dp", None), P("dp"), P("lat", None, None)),
        out_specs=(spec, P("dp", None), P("dp", None), P("dp"), P("lat", None, None)),
        check_vma=False,
    )
```

```python
import functools
import math

import jax
import jax.numpy as jnp
import numpy as np
from jax import lax
from jax.experimental import pallas as pl
from jax.experimental.pallas import tpu as pltpu
from jax.sharding import PartitionSpec as P

C = 192
H = 6
HD = 32
WZ = 2
WA = 6
WL = 12
SA = 3
SO = 6
WT = 144
POS = 3312
EPS = 1e-05
MASKED = -1e30

ROWS = WZ * WA
SPAN = 2 * WL - 1
QUAD = WZ * SA * 8
WIDE = 256
LEAD = 11 * SPAN
HALO = 3 * QUAD // 2
TABLE = H * ROWS + 16
BF = jnp.bfloat16
F32 = jnp.float32
VMEM = pl.BlockSpec(memory_space=pltpu.VMEM)


def dp_index():
    return lax.axis_index("dp")


def side_index():
    column = lax.axis_index("lon")
    return lax.rem(column + lax.div(column, 2), 2)


def last_row():
    return lax.axis_index("lat") == lax.axis_size("lat") - 1


def token_order():
    order = np.zeros((WT, 4 * QUAD), np.float32)
    for z in range(WZ):
        for a in range(WA):
            for o in range(WL):
                south, east = a >= SA, o >= SO
                quadrant = 2 * south + east
                column = o - SO if east else o + 2
                row = (z * SA + a % SA) * 8 + column
                order[(z * WA + a) * WL + o, quadrant * QUAD + row] = 1.0
    return order


def matmul(a, b):
    return lax.dot_general(a, b, (((1,), (0,)), ((), ())), preferred_element_type=F32)


def matmul_t(a, b):
    return lax.dot_general(a, b, (((1,), (1,)), ((), ())), preferred_element_type=F32)


def over_12(index):
    return lax.shift_right_logical(index * 5462, 16)


def spread_lanes(row, position, parts):
    width = row.shape[1]
    full = jnp.zeros((1, C), F32)
    for k in range(parts):
        pieces = [row]
        if k:
            pieces.insert(0, jnp.zeros((1, k * width), F32))
        if k < parts - 1:
            pieces.append(jnp.zeros((1, (parts - 1 - k) * width), F32))
        full = jnp.where(position == k, jnp.concatenate(pieces, axis=1), full)
    return full


def folded(value):
    rows = value.shape[0]
    top, tail = value[: 3 * rows // 4], value[3 * rows // 4 :]
    side = jnp.concatenate([tail[:, at : at + 64] for at in (0, 64, 128)], axis=0)
    return jnp.concatenate([top, side], axis=1)


def unfolded(value):
    rows = value.shape[0] // 3
    side = value[:, C:]
    tail = jnp.concatenate([side[k * rows : (k + 1) * rows] for k in range(3)], axis=1)
    return jnp.concatenate([value[:, :C], tail], axis=0)


def pack_kernel(parts, tok, dy, qkv, proj, gain, dense, east, south, corner):
    n_qkv, n_proj = 3 * C // parts, C // parts
    dense[:n_qkv] = qkv[...]
    dense[n_qkv : n_qkv + n_proj] = proj[...]
    row = spread_lanes(gain[...].astype(F32), dp_index(), parts)
    dense[n_qkv + n_proj :] = jnp.broadcast_to(row, (16, C)).astype(BF)

    def strips(rows, cols):
        pair = []
        for ref in (tok, dy):
            part = ref[:, rows : rows + SA].astype(F32)
            pair.append(part[:, :, cols : cols + 8].reshape(QUAD, C))
        return folded(jnp.concatenate(pair, axis=0)).astype(BF)

    east[...] = strips(SA, 0)
    south[...] = strips(0, 4)
    corner[...] = strips(0, 0)


def offsets(height, width, half):
    row = lax.broadcasted_iota(jnp.int32, (height, width), 0)
    col = lax.broadcasted_iota(jnp.int32, (height, width), 1)
    block = over_12(col)
    return row, block * SPAN - (col - block * WL) + WL - 1 - half


def bias_kernel(table, out):
    values = table[...]
    high = values.astype(BF)
    rest = values - high.astype(F32)
    middle = rest.astype(BF)
    low = (rest - middle.astype(F32)).astype(BF)
    stacked = jnp.concatenate([high, middle, low], axis=0)
    row, target = offsets(ROWS * SPAN, WIDE, 0)
    count = H * ROWS
    here = lax.broadcasted_iota(jnp.int32, (count, WIDE), 0)
    here = here - over_12(here) * ROWS
    there = over_12(lax.broadcasted_iota(jnp.int32, (count, WIDE), 1))

    def wrapped(index):
        return jnp.where(index >= WA, index - WA, index) >= SA

    crossing = jnp.logical_and(wrapped(here) != wrapped(there), last_row())
    for u in range(WL):
        onehot = jnp.where(row == target + u, 1.0, 0.0).astype(BF)
        spread = matmul(stacked, onehot)
        spread = spread[:count] + spread[count : 2 * count] + spread[2 * count :]
        spread = jnp.where(crossing, MASKED, spread)
        out[0, pl.ds(u, count, stride=WL), :] = spread[:, :128]
        out[1, pl.ds(u, count, stride=WL), :] = spread[:, 128:]


def main_kernel(
    parts, pieces, south, corner, east, tok, dy, bias, order, *refs
):
    dense = refs[:parts]
    send, keep, gain_sum, scores_grad, grad_qkv, unit_out, scale_out, qkv_w, proj_w, sums = refs[parts:]
    n_qkv, n_proj = 3 * C // parts, C // parts
    gain = None
    for k in range(parts):
        at = lax.rem(dp_index() + k, parts)
        qkv_w[pl.ds(pl.multiple_of(at * n_qkv, 16), n_qkv), :] = dense[k][:n_qkv]
        proj_w[pl.ds(pl.multiple_of(at * n_proj, 16), n_proj), :] = dense[k][n_qkv : n_qkv + n_proj]
        term = dense[k][n_qkv + n_proj : n_qkv + n_proj + 16].astype(F32)[:1]
        gain = term if gain is None else gain + term

    def own(ref):
        part = ref[:, SA:].astype(F32)
        return part[:, :, 4:12].reshape(QUAD, C).astype(BF)

    halos = [unfolded(ref[...].astype(F32)).astype(BF) for ref in (east, south, corner)]

    def window(ref, index):
        at = slice(index * QUAD, (index + 1) * QUAD)
        return jnp.concatenate([own(ref)] + [halo[at] for halo in halos], axis=0)

    x = matmul(order[...], window(tok, 0))
    dyw = matmul(order[...], window(dy, 1)).astype(BF)
    average = jnp.sum(x, axis=-1, keepdims=True) * (1.0 / C)
    centred = x - average
    variance = jnp.sum(centred * centred, axis=-1, keepdims=True) * (1.0 / C)
    inverse = lax.rsqrt(variance + EPS)
    unit = centred * inverse
    normed = (unit * gain).astype(BF)
    qkv_t = matmul_t(qkv_w[...], normed).astype(BF)
    query = matmul_t(normed, qkv_w[:C]).astype(BF)
    grad_att32 = matmul(dyw, proj_w[...]).astype(BF).astype(F32)
    grad_att = grad_att32.astype(BF)
    grad_att_t = grad_att32.T.astype(BF)
    dy_t = dyw.astype(F32).T.astype(BF)
    scale = 1.0 / math.sqrt(HD)

    def both(ref, at):
        rows = slice(at, at + WT)
        return jnp.concatenate([ref[0, rows], ref[1, rows, : WT - 128]], axis=1)

    attended_t, grad_q, grad_k, grad_v = [], [], [], []
    for group in range(0, H, 6):
        heads = range(group, group + 6)
        spans = [slice(head * HD, (head + 1) * HD) for head in heads]
        q_t = [qkv_t[span] for span in spans]
        k_t = [qkv_t[C:][span] for span in spans]
        v_t = [qkv_t[2 * C :][span] for span in spans]
        scores = [
            matmul(query[:, span], k) * scale + both(bias, head * WT)
            for head, span, k in zip(heads, spans, k_t)
        ]
        grad_probs = [matmul(grad_att[:, span], v) for span, v in zip(spans, v_t)]
        expo = [jnp.exp(s - jnp.max(s, axis=-1, keepdims=True)) for s in scores]
        probs = [e * (1.0 / jnp.sum(e, axis=-1, keepdims=True)) for e in expo]
        probs_low = [p.astype(BF) for p in probs]
        means = [jnp.sum(p * g, axis=-1, keepdims=True) for p, g in zip(probs, grad_probs)]
        grad_scores = [p * (g - m) for p, g, m in zip(probs, grad_probs, means)]
        scores_low = [g.astype(BF) for g in grad_scores]
        attended_t += [matmul_t(v, p) for v, p in zip(v_t, probs_low)]
        grad_v += [matmul(grad_att_t[span], p) for span, p in zip(spans, probs_low)]
        grad_q += [matmul_t(k, g) * scale for k, g in zip(k_t, scores_low)]
        grad_k += [matmul(q, g) * scale for q, g in zip(q_t, scores_low)]
        for head, value in zip(heads, grad_scores):
            scores_grad[0, head * WT : (head + 1) * WT] = value[:, :128]
            scores_grad[1, head * WT : (head + 1) * WT, : WT - 128] = value[:, 128:]
    grad_qkv_t32 = jnp.concatenate(grad_q + grad_k + grad_v, axis=0)
    grad_qkv_t = grad_qkv_t32.astype(BF)
    grad_qkv_w = matmul(grad_qkv_t, normed)
    grad_proj = matmul_t(dy_t, jnp.concatenate(attended_t, axis=0).astype(BF))
    each = n_qkv + n_proj
    for k in range(parts):
        sums[k * each : k * each + n_qkv] = grad_qkv_w[k * n_qkv : (k + 1) * n_qkv]
        sums[k * each + n_qkv : (k + 1) * each] = grad_proj[k * n_proj : (k + 1) * n_proj]
    half = each // 2
    size = half // pieces
    for k in range(parts):
        for p in range(pieces):
            mine = k * each + side_index() * half + p * size
            other = k * each + (1 - side_index()) * half + p * size
            at = (k * pieces + p) * 3 * size // 4
            rows = slice(at, at + 3 * size // 4)
            keep[rows] = folded(sums[pl.ds(pl.multiple_of(mine, 16), size), :])
            send[rows] = folded(sums[pl.ds(pl.multiple_of(other, 16), size), :]).astype(BF)
    weighted = jnp.sum(grad_qkv_w * qkv_w[...].astype(F32), axis=0, keepdims=True)
    gain_sum[...] = jnp.broadcast_to(weighted / gain, (8, C))
    grad_qkv[...] = grad_qkv_t32
    unit_out[...] = unit
    scale_out[:WT] = jnp.broadcast_to(inverse, (WT, C))
    scale_out[WT:] = jnp.broadcast_to(gain, (16, C))


def table_kernel(scores_grad, table):
    count = H * ROWS
    row, target = offsets(288, WT, 0)
    total = jnp.zeros((count, 288), F32)
    for u in range(WL):
        onehot = jnp.where(row == target + u, 1.0, 0.0).astype(BF)
        rows = pl.ds(u, count, stride=WL)
        wide = jnp.concatenate(
            [scores_grad[0, rows, :], scores_grad[1, rows, :][:, : WT - 128]], axis=1
        )
        total += matmul_t(wide.astype(BF), onehot)
    tail = total[:, LEAD : LEAD + SPAN]
    tail = jnp.concatenate([tail[h * ROWS : (h + 1) * ROWS] for h in range(H)], axis=1)
    tail = jnp.concatenate([tail, jnp.zeros((ROWS, WIDE - H * SPAN), F32)], axis=1)
    rest = jnp.zeros((16 - ROWS, WIDE), F32)
    table[...] = jnp.concatenate([total[:, :WIDE], tail, rest], axis=0).astype(BF)


def token_kernel(grad_qkv_t, unit, scales, qkv_w, order_t, quads, south):
    grad_normed = matmul(grad_qkv_t[...].T.astype(BF), qkv_w[...])
    inverse = scales[:WT]
    scaled = grad_normed * scales[WT : WT + 1]
    first = jnp.sum(scaled, axis=-1, keepdims=True) * (1.0 / C)
    second = jnp.sum(scaled * unit[...], axis=-1, keepdims=True) * (1.0 / C)
    grad_x = inverse * (scaled - first - unit[...] * second)
    every = matmul(order_t[...], grad_x.astype(BF))
    quads[...] = every[: 2 * QUAD].astype(BF)
    south[...] = folded(every[2 * QUAD :]).astype(BF)


def east_kernel(quads, south, east):
    corner = unfolded(south[...].astype(F32))[QUAD:]
    east[...] = folded(jnp.concatenate([quads[QUAD:].astype(F32), corner], axis=0)).astype(BF)


def finish_kernel(dy, quads, south, east, out, out_s, sem):
    gap = jnp.zeros((4, C), F32)
    lon_halo = unfolded(east[...].astype(F32))
    lat_halo = unfolded(south[...].astype(F32))[:QUAD]
    mine = quads[:QUAD].astype(F32)
    levels = []
    for z in range(WZ):
        rows = []
        for a in range(WA):
            at = (z * SA + a % SA) * 8
            low = lon_halo[at : at + 8] if a >= SA else lon_halo[QUAD + at : QUAD + at + 8]
            high = mine[at : at + 8] if a >= SA else lat_halo[at : at + 8]
            low, high = jnp.concatenate([low, gap]), jnp.concatenate([gap, high])
            rows.append(dy[z, a].astype(F32) + low + high)
        levels.append(jnp.concatenate(rows, axis=0))
    out_s[...] = jnp.stack(levels, axis=1).astype(BF)
    copy = pltpu.make_async_copy(out_s, out, sem)
    copy.start()
    copy.wait()


def widened(rows):
    return jnp.concatenate([rows, jnp.zeros((rows.shape[0], WIDE - C), F32)], axis=1)


def chip_index():
    return lax.div(lax.axis_index("lon"), 2)


def plane_kernel(keep, got, gain_sum, table, mine, to_dp, to_lon, to_both):
    rows = keep.shape[0] // 4

    def piece(other_dp, other_chip):
        dp = dp_index() if not other_dp else 1 - dp_index()
        chip = chip_index() if not other_chip else 1 - chip_index()
        at = pl.ds(pl.multiple_of((2 * dp + chip) * rows, 8), rows)
        return keep[at, :] + got[at, :].astype(F32)

    mine[...] = piece(False, False)
    to_dp[...] = jnp.concatenate(
        [piece(True, False), widened(gain_sum[...]), table[...].astype(F32)], axis=0
    ).astype(BF)
    to_lon[...] = piece(False, True).astype(BF)
    to_both[...] = piece(True, True).astype(BF)


def plane_sum_kernel(mine, sent, from_both, from_dp, from_lon, halo, out, table):
    rows = mine.shape[0]
    got = from_dp[...].astype(F32)
    dense = mine[...] + got[:rows] + from_lon[...].astype(F32) + from_both[...].astype(F32)
    shared = sent[...].astype(F32)[rows:] + got[rows:]
    out[...] = jnp.concatenate([dense, shared[:8], halo[...].astype(F32)], axis=0).astype(BF)
    table[...] = shared[8:].astype(BF)


def sum_kernel(sent, got, out):
    out[...] = (sent[...].astype(F32) + got[...].astype(F32)).astype(BF)


def relay_kernel(sent, got, out):
    sent, got = sent[...].astype(F32), got[...].astype(F32)
    rows = sent.shape[0] - HALO
    out[...] = jnp.concatenate([sent[:rows] + got[:rows], sent[rows:]], axis=0).astype(BF)


def lon_kernel(sent, got, before, quads, out, south, east):
    sent, got = sent[...].astype(F32), got[...].astype(F32)
    rows = sent.shape[0] - HALO
    halo = jnp.where(
        lax.rem(lax.axis_index("lat"), 2) == 1, before[...].astype(F32)[rows:], got[rows:]
    )
    south[...] = halo.astype(BF)
    corner = unfolded(halo)[QUAD:]
    halo = folded(jnp.concatenate([quads[QUAD:].astype(F32), corner], axis=0))
    east[...] = halo.astype(BF)
    out[...] = jnp.concatenate([sent[:rows] + got[:rows], halo], axis=0).astype(BF)


def join_kernel(sent, got, out):
    sent, got = sent[...].astype(F32), got[...].astype(F32)
    rows = sent.shape[0] - HALO - 8
    first = chip_index() == 0
    low = jnp.where(first, sent[:rows], got[:rows])
    high = jnp.where(first, got[:rows], sent[:rows])
    gain_sum = sent[rows : rows + 8] + got[rows : rows + 8]
    out[...] = jnp.concatenate([low, high, gain_sum], axis=0).astype(BF)


def choose_kernel(got, earlier, out):
    rows = earlier.shape[0] - HALO
    earlier = earlier[...].astype(F32)[rows:]
    odd = lax.rem(lax.axis_index("lon"), 2) == 1
    out[...] = jnp.where(odd, got[...].astype(F32), earlier).astype(BF)


def last_kernel(
    sent, got, table_sent, table_got, qkv_out, proj_out, gain_out, table_out,
    dense_s, gain_s, table_s, sems,
):
    sent, got = sent[...].astype(F32), got[...].astype(F32)
    rows = (sent.shape[0] - 8) // 2
    size = 4 * rows // 3
    gain_sum = sent[2 * rows : 2 * rows + 1] + got[2 * rows : 2 * rows + 1]
    gain_s[...] = jnp.where(dp_index() == 0, gain_sum[:, : C // 2], gain_sum[:, C // 2 : C])
    for side, value in ((side_index(), sent), (1 - side_index(), got)):
        for p in range(2):
            at = pl.ds(pl.multiple_of((2 * side + p) * size, 16), size)
            dense_s[at, :] = unfolded(value[p * rows : (p + 1) * rows])
    copies = [
        pltpu.make_async_copy(dense_s.at[: 3 * size], qkv_out, sems.at[0]),
        pltpu.make_async_copy(dense_s.at[3 * size :], proj_out, sems.at[1]),
        pltpu.make_async_copy(gain_s, gain_out, sems.at[2]),
        pltpu.make_async_copy(table_s, table_out, sems.at[3]),
    ]
    for copy in copies[:3]:
        copy.start()
    table = table_sent[...].astype(F32) + table_got[...].astype(F32)
    count = H * ROWS
    tail = table[count : count + ROWS]
    tail = jnp.concatenate([tail[:, h * SPAN : (h + 1) * SPAN] for h in range(H)], axis=0)
    table = jnp.concatenate([table[:count, :LEAD], tail], axis=1)
    for h in range(H):
        rows = [table[h * ROWS + a : h * ROWS + a + 1] for a in range(ROWS)]
        table_s[h] = jnp.concatenate(rows, axis=1)
    copies[3].start()
    for copy in copies:
        copy.wait()


def call(kernel, outs, scratch=(), specs=None, flops=1000000, nbytes=1000000, out_specs=None):
    return pl.pallas_call(
        kernel,
        out_shape=outs,
        in_specs=specs,
        out_specs=jax.tree.map(lambda _: VMEM, outs) if out_specs is None else out_specs,
        scratch_shapes=list(scratch),
        compiler_params=pltpu.CompilerParams(vmem_limit_bytes=24 << 20),
        cost_estimate=pl.CostEstimate(flops=flops, bytes_accessed=nbytes, transcendentals=0),
    )


def shaped(rows, cols, dtype):
    return jax.ShapeDtypeStruct((rows, cols), dtype)


def exchanged(value, axis, flip):
    count = lax.axis_size(axis)
    return lax.ppermute(value, axis, [(i, i ^ flip) for i in range(count)])


def exchanged_both(value):
    pairs = [(2 * i + k, 2 * (i ^ 3) + (1 - k)) for i in range(4) for k in range(2)]
    return lax.ppermute(value, ("lon", "dp"), pairs)


def tied(*values):
    return lax.optimization_barrier(values)


def passed_along(value, axis, steps):
    count = lax.axis_size(axis)
    return lax.ppermute(value, axis, [(i, (i + steps) % count) for i in range(count)])


def passed_diagonally(value, steps):
    rows, cols = lax.axis_size("lon"), lax.axis_size("lat")
    pairs = [
        (i * cols + j, ((i + steps) % rows) * cols + (j + steps) % cols)
        for i in range(rows)
        for j in range(cols)
    ]
    return lax.ppermute(value, ("lon", "lat"), pairs)


def body(tokens, grad_out, qkv_weight, proj_weight, norm_gain, bias_table):
    parts = lax.axis_size("dp")
    lon_count, lat_count = lax.axis_size("lon"), lax.axis_size("lat")
    fast = (lon_count, lat_count, parts) == (4, 4, 2)
    n_qkv, n_proj = 3 * C // parts, C // parts
    each = n_qkv + n_proj
    half = each // 2
    tok = tokens.reshape(WZ, WA, WL, C)
    dy = grad_out.reshape(WZ, WA, WL, C)

    strips = [shaped(HALO, WIDE, BF)] * 3
    dense, east, south, corner = call(
        functools.partial(pack_kernel, parts), [shaped(each + 16, C, BF)] + strips, specs=[VMEM] * 5
    )(tok, dy, qkv_weight, proj_weight, norm_gain.reshape(1, n_proj))
    gathered = [dense] + [passed_along(dense, "dp", -k) for k in range(1, parts)]
    south = passed_along(south, "lat", -1)
    corner = passed_diagonally(corner, -1)
    east = passed_along(east, "lon", -1)
    bias = call(
        bias_kernel,
        jax.ShapeDtypeStruct((2, H * WT, 128), F32),
        specs=[VMEM],
        flops=200000000,
    )(bias_table.reshape(H * ROWS, ROWS * SPAN))
    order = token_order()
    packed = parts * 3 * half // 4
    outs = [
        shaped(packed, WIDE, BF),
        shaped(packed, WIDE, F32),
        shaped(8, C, F32),
        jax.ShapeDtypeStruct((2, H * WT, 128), F32),
        shaped(3 * C, WT, F32),
        shaped(WT, C, F32),
        shaped(WT + 16, C, F32),
        shaped(3 * C, C, BF),
    ]
    scratch = [pltpu.VMEM((C, C), BF), pltpu.VMEM((4 * C, C), F32)]
    send, keep, gain_sum, scores_grad, grad_qkv, unit, scales, qkv_full = call(
        functools.partial(main_kernel, parts, 2 if fast else 1),
        outs,
        scratch,
        specs=[VMEM] * (7 + parts),
    )(south, corner, east, tok, dy, bias, jnp.asarray(order, BF), *gathered)
    if fast:
        got = exchanged(send, "lon", 1)
    table = call(table_kernel, shaped(TABLE, WIDE, BF), specs=[VMEM], flops=200000000)(scores_grad)
    if fast:
        piece = packed // 4
        mine, sent, to_lon, to_both = call(
            plane_kernel,
            [
                shaped(piece, WIDE, F32),
                shaped(piece + 8 + TABLE, WIDE, BF),
                shaped(piece, WIDE, BF),
                shaped(piece, WIDE, BF),
            ],
            specs=[VMEM] * 4,
        )(keep, got, gain_sum, table)
        from_both = exchanged_both(to_both)
        got = exchanged(sent, "dp", 1)
        from_lon = exchanged(to_lon, "lon", 3)
    quads, south = call(
        token_kernel,
        [shaped(2 * QUAD, C, BF), shaped(HALO, WIDE, BF)],
        specs=[VMEM] * 5,
        flops=100000000,
    )(grad_qkv, unit, scales, qkv_full, jnp.asarray(order.T, BF))
    if fast:
        lat_shape = shaped(piece + 8 + HALO, WIDE, BF)
        table_shape = shaped(TABLE, WIDE, BF)
        halo_shape = shaped(HALO, WIDE, BF)
        sent, table = call(plane_sum_kernel, [lat_shape, table_shape], specs=[VMEM] * 6)(
            mine, sent, from_both, got, from_lon, south
        )
        before = exchanged(sent, "lat", 1)
        sent = call(relay_kernel, lat_shape, specs=[VMEM] * 2)(sent, before)
        sent, table = tied(sent, table)
        got = exchanged(sent, "lat", 3)
        table_got = exchanged(table, "lon", 3)
        sent, south, east = call(
            lon_kernel, [lat_shape, halo_shape, halo_shape], specs=[VMEM] * 4
        )(sent, got, before, quads)
        sent, table_got = tied(sent, table_got)
        got = exchanged(sent, "lon", 3)
        table = call(sum_kernel, table_shape, specs=[VMEM] * 2)(table, table_got)
        table_got = exchanged(table, "lon", 1)
        east_got = exchanged(east, "lon", 1)
        east = call(choose_kernel, halo_shape, specs=[VMEM] * 2)(east_got, got)
    else:
        south = passed_along(south, "lat", 1)
        east = call(east_kernel, shaped(HALO, WIDE, BF), specs=[VMEM] * 2)(quads, south)
        east = passed_along(east, "lon", 1)
    hbm = pl.BlockSpec(memory_space=pltpu.HBM)
    tile = (WA * WL, WZ, C)
    finish = call(
        finish_kernel,
        jax.ShapeDtypeStruct(tile, BF),
        [pltpu.VMEM(tile, BF), pltpu.SemaphoreType.DMA],
        specs=[VMEM] * 4,
        out_specs=hbm,
    )

    def tokens_of(columns):
        return columns.reshape(WA, WL, WZ, C).transpose(2, 0, 1, 3)[None]

    if fast:
        sent = call(join_kernel, shaped(2 * piece + 8, WIDE, BF), specs=[VMEM] * 2)(sent, got)
        sent, table_got, east = tied(sent, table_got, east)
        got = exchanged(sent, "lon", 1)
        grad_tokens = finish(dy, quads, south, east)
        got, grad_tokens = tied(got, grad_tokens)
        grad_tokens = tokens_of(grad_tokens)
        grad_qkv_w, grad_proj, grad_gain, grad_table = call(
            last_kernel,
            [
                shaped(n_qkv, C, F32),
                shaped(n_proj, C, F32),
                shaped(1, n_proj, F32),
                jax.ShapeDtypeStruct((H, 1, POS), F32),
            ],
            [
                pltpu.VMEM((each, C), F32),
                pltpu.VMEM((1, n_proj), F32),
                pltpu.VMEM((H, 1, POS), F32),
                pltpu.SemaphoreType.DMA((4,)),
            ],
            specs=[VMEM] * 4,
            out_specs=[hbm] * 4,
        )(sent, got, table, table_got)
        grad_gain, grad_table = grad_gain.reshape(n_proj), grad_table.reshape(1, H, POS)
        return grad_tokens, grad_qkv_w, grad_proj, grad_gain, grad_table
    grad_tokens = tokens_of(finish(dy, quads, south, east))
    pair = jnp.stack([keep, send.astype(F32)]).reshape(2, parts, packed // parts, WIDE)
    pair = jnp.where(side_index() == 0, pair, pair[::-1])
    pair = jax.vmap(jax.vmap(unfolded))(pair)
    dense_sum = lax.psum(pair.transpose(1, 0, 2, 3).reshape(parts * each, C), ("lon", "lat"))
    total = lax.psum_scatter(dense_sum, "dp", scatter_dimension=0, tiled=True)
    grad_gain = lax.psum(gain_sum[0], ("lon", "lat"))
    grad_gain = lax.psum_scatter(grad_gain, "dp", scatter_dimension=0, tiled=True)
    table = lax.psum(table.astype(F32), ("lon", "dp"))
    count = H * ROWS
    tail = table[count : count + ROWS, : H * SPAN].reshape(ROWS, H, SPAN)
    tail = tail.transpose(1, 0, 2).reshape(count, SPAN)
    table = jnp.concatenate([table[:count, :LEAD], tail], axis=1)
    return (
        grad_tokens,
        total[:n_qkv],
        total[n_qkv:],
        grad_gain,
        table.reshape(1, H, POS),
    )


def solution(mesh):
    spec = P("dp", None, "lat", "lon", None)
    return jax.shard_map(
        body,
        mesh=mesh,
        in_specs=(spec, spec, P("dp", None), P("dp", None), P("dp"), P("lat", None, None)),
        out_specs=(spec, P("dp", None), P("dp", None), P("dp"), P("lat", None, None)),
        check_vma=False,
    )
```

```python
import functools
import math

import jax
import jax.numpy as jnp
import numpy as np
from jax import lax
from jax.experimental import pallas as pl
from jax.experimental.pallas import tpu as pltpu
from jax.sharding import PartitionSpec as P

C = 192
H = 6
HD = 32
WZ = 2
WA = 6
WL = 12
SA = 3
SO = 6
WT = 144
POS = 3312
EPS = 1e-05
MASKED = -1e30

ROWS = WZ * WA
SPAN = 2 * WL - 1
QUAD = WZ * SA * 8
WIDE = 256
LEAD = 11 * SPAN
HALO = 3 * QUAD // 2
TABLE = H * ROWS + 16
BF = jnp.bfloat16
F32 = jnp.float32
VMEM = pl.BlockSpec(memory_space=pltpu.VMEM)


def dp_index():
    return lax.axis_index("dp")


def side_index():
    column = lax.axis_index("lon")
    return lax.rem(column + lax.div(column, 2), 2)


def last_row():
    return lax.axis_index("lat") == lax.axis_size("lat") - 1


def token_order():
    order = np.zeros((WT, 4 * QUAD), np.float32)
    for z in range(WZ):
        for a in range(WA):
            for o in range(WL):
                south, east = a >= SA, o >= SO
                quadrant = 2 * south + east
                column = o - SO if east else o + 2
                row = (z * SA + a % SA) * 8 + column
                order[(z * WA + a) * WL + o, quadrant * QUAD + row] = 1.0
    return order


def matmul(a, b):
    return lax.dot_general(a, b, (((1,), (0,)), ((), ())), preferred_element_type=F32)


def matmul_t(a, b):
    return lax.dot_general(a, b, (((1,), (1,)), ((), ())), preferred_element_type=F32)


def over_12(index):
    return lax.shift_right_logical(index * 5462, 16)


def spread_lanes(row, position, parts):
    width = row.shape[1]
    full = jnp.zeros((1, C), F32)
    for k in range(parts):
        pieces = [row]
        if k:
            pieces.insert(0, jnp.zeros((1, k * width), F32))
        if k < parts - 1:
            pieces.append(jnp.zeros((1, (parts - 1 - k) * width), F32))
        full = jnp.where(position == k, jnp.concatenate(pieces, axis=1), full)
    return full


def folded(value):
    rows = value.shape[0]
    top, tail = value[: 3 * rows // 4], value[3 * rows // 4 :]
    side = jnp.concatenate([tail[:, at : at + 64] for at in (0, 64, 128)], axis=0)
    return jnp.concatenate([top, side], axis=1)


def unfolded(value):
    rows = value.shape[0] // 3
    side = value[:, C:]
    tail = jnp.concatenate([side[k * rows : (k + 1) * rows] for k in range(3)], axis=1)
    return jnp.concatenate([value[:, :C], tail], axis=0)


def pack_kernel(parts, tok, dy, qkv, proj, gain, dense, east, south, corner):
    n_qkv, n_proj = 3 * C // parts, C // parts
    dense[:n_qkv] = qkv[...]
    dense[n_qkv : n_qkv + n_proj] = proj[...]
    row = spread_lanes(gain[...].astype(F32), dp_index(), parts)
    dense[n_qkv + n_proj :] = jnp.broadcast_to(row, (16, C)).astype(BF)

    def strips(rows, cols):
        pair = []
        for ref in (tok, dy):
            part = ref[:, rows : rows + SA].astype(F32)
            pair.append(part[:, :, cols : cols + 8].reshape(QUAD, C))
        return folded(jnp.concatenate(pair, axis=0)).astype(BF)

    east[...] = strips(SA, 0)
    south[...] = strips(0, 4)
    corner[...] = strips(0, 0)


def offsets(height, width, half):
    row = lax.broadcasted_iota(jnp.int32, (height, width), 0)
    col = lax.broadcasted_iota(jnp.int32, (height, width), 1)
    block = over_12(col)
    return row, block * SPAN - (col - block * WL) + WL - 1 - half


def bias_kernel(table, out):
    values = table[...]
    high = values.astype(BF)
    rest = values - high.astype(F32)
    middle = rest.astype(BF)
    low = (rest - middle.astype(F32)).astype(BF)
    stacked = jnp.concatenate([high, middle, low], axis=0)
    row, target = offsets(ROWS * SPAN, WIDE, 0)
    count = H * ROWS
    here = lax.broadcasted_iota(jnp.int32, (count, WIDE), 0)
    here = here - over_12(here) * ROWS
    there = over_12(lax.broadcasted_iota(jnp.int32, (count, WIDE), 1))

    def wrapped(index):
        return jnp.where(index >= WA, index - WA, index) >= SA

    crossing = jnp.logical_and(wrapped(here) != wrapped(there), last_row())
    for u in range(WL):
        onehot = jnp.where(row == target + u, 1.0, 0.0).astype(BF)
        spread = matmul(stacked, onehot)
        spread = spread[:count] + spread[count : 2 * count] + spread[2 * count :]
        spread = jnp.where(crossing, MASKED, spread)
        out[0, pl.ds(u, count, stride=WL), :] = spread[:, :128]
        out[1, pl.ds(u, count, stride=WL), :] = spread[:, 128:]


def main_kernel(
    parts, pieces, south, corner, east, tok, dy, bias, order, *refs
):
    dense = refs[:parts]
    send, keep, gain_sum, scores_grad, grad_qkv, unit_out, scale_out, qkv_w, proj_w, sums = refs[parts:]
    n_qkv, n_proj = 3 * C // parts, C // parts
    gain = None
    for k in range(parts):
        at = lax.rem(dp_index() + k, parts)
        qkv_w[pl.ds(pl.multiple_of(at * n_qkv, 16), n_qkv), :] = dense[k][:n_qkv]
        proj_w[pl.ds(pl.multiple_of(at * n_proj, 16), n_proj), :] = dense[k][n_qkv : n_qkv + n_proj]
        term = dense[k][n_qkv + n_proj : n_qkv + n_proj + 16].astype(F32)[:1]
        gain = term if gain is None else gain + term

    def own(ref):
        part = ref[:, SA:].astype(F32)
        return part[:, :, 4:12].reshape(QUAD, C).astype(BF)

    halos = [unfolded(ref[...].astype(F32)).astype(BF) for ref in (east, south, corner)]

    def window(ref, index):
        at = slice(index * QUAD, (index + 1) * QUAD)
        return jnp.concatenate([own(ref)] + [halo[at] for halo in halos], axis=0)

    x = matmul(order[...], window(tok, 0))
    dyw = matmul(order[...], window(dy, 1)).astype(BF)
    average = jnp.sum(x, axis=-1, keepdims=True) * (1.0 / C)
    centred = x - average
    variance = jnp.sum(centred * centred, axis=-1, keepdims=True) * (1.0 / C)
    inverse = lax.rsqrt(variance + EPS)
    unit = centred * inverse
    normed = (unit * gain).astype(BF)
    qkv_t = matmul_t(qkv_w[...], normed).astype(BF)
    query = matmul_t(normed, qkv_w[:C]).astype(BF)
    grad_att32 = matmul(dyw, proj_w[...]).astype(BF).astype(F32)
    grad_att = grad_att32.astype(BF)
    grad_att_t = grad_att32.T.astype(BF)
    dy_t = dyw.astype(F32).T.astype(BF)
    scale = 1.0 / math.sqrt(HD)

    def both(ref, at):
        rows = slice(at, at + WT)
        return jnp.concatenate([ref[0, rows], ref[1, rows, : WT - 128]], axis=1)

    attended_t, grad_q, grad_k, grad_v = [], [], [], []
    for group in range(0, H, 6):
        heads = range(group, group + 6)
        spans = [slice(head * HD, (head + 1) * HD) for head in heads]
        q_t = [qkv_t[span] for span in spans]
        k_t = [qkv_t[C:][span] for span in spans]
        v_t = [qkv_t[2 * C :][span] for span in spans]
        scores = [
            matmul(query[:, span], k) * scale + both(bias, head * WT)
            for head, span, k in zip(heads, spans, k_t)
        ]
        grad_probs = [matmul(grad_att[:, span], v) for span, v in zip(spans, v_t)]
        expo = [jnp.exp(s - jnp.max(s, axis=-1, keepdims=True)) for s in scores]
        probs = [e * (1.0 / jnp.sum(e, axis=-1, keepdims=True)) for e in expo]
        probs_low = [p.astype(BF) for p in probs]
        means = [jnp.sum(p * g, axis=-1, keepdims=True) for p, g in zip(probs, grad_probs)]
        grad_scores = [p * (g - m) for p, g, m in zip(probs, grad_probs, means)]
        scores_low = [g.astype(BF) for g in grad_scores]
        attended_t += [matmul_t(v, p) for v, p in zip(v_t, probs_low)]
        grad_v += [matmul(grad_att_t[span], p) for span, p in zip(spans, probs_low)]
        grad_q += [matmul_t(k, g) * scale for k, g in zip(k_t, scores_low)]
        grad_k += [matmul(q, g) * scale for q, g in zip(q_t, scores_low)]
        for head, value in zip(heads, grad_scores):
            scores_grad[0, head * WT : (head + 1) * WT] = value[:, :128]
            scores_grad[1, head * WT : (head + 1) * WT, : WT - 128] = value[:, 128:]
    grad_qkv_t32 = jnp.concatenate(grad_q + grad_k + grad_v, axis=0)
    grad_qkv_t = grad_qkv_t32.astype(BF)
    grad_qkv_w = matmul(grad_qkv_t, normed)
    grad_proj = matmul_t(dy_t, jnp.concatenate(attended_t, axis=0).astype(BF))
    each = n_qkv + n_proj
    for k in range(parts):
        sums[k * each : k * each + n_qkv] = grad_qkv_w[k * n_qkv : (k + 1) * n_qkv]
        sums[k * each + n_qkv : (k + 1) * each] = grad_proj[k * n_proj : (k + 1) * n_proj]
    half = each // 2
    size = half // pieces
    for k in range(parts):
        for p in range(pieces):
            mine = k * each + side_index() * half + p * size
            other = k * each + (1 - side_index()) * half + p * size
            at = (k * pieces + p) * 3 * size // 4
            rows = slice(at, at + 3 * size // 4)
            keep[rows] = folded(sums[pl.ds(pl.multiple_of(mine, 16), size), :])
            send[rows] = folded(sums[pl.ds(pl.multiple_of(other, 16), size), :]).astype(BF)
    weighted = jnp.sum(grad_qkv_w * qkv_w[...].astype(F32), axis=0, keepdims=True)
    gain_sum[...] = jnp.broadcast_to(weighted / gain, (8, C))
    grad_qkv[...] = grad_qkv_t32
    unit_out[...] = unit
    scale_out[:WT] = jnp.broadcast_to(inverse, (WT, C))
    scale_out[WT:] = jnp.broadcast_to(gain, (16, C))


def table_kernel(scores_grad, table):
    count = H * ROWS
    row, target = offsets(288, WT, 0)
    onehots = [jnp.where(row == target + u, 1.0, 0.0).astype(BF) for u in range(WL)]
    strides = [pl.ds(u, count, stride=WL) for u in range(WL)]
    wide = [
        jnp.concatenate([scores_grad[0, rows, :], scores_grad[1, rows, :][:, : WT - 128]], axis=1)
        for rows in strides
    ]
    terms = [matmul_t(value.astype(BF), onehot) for value, onehot in zip(wide, onehots)]
    while len(terms) > 1:
        pairs = [sum(terms[k : k + 2]) for k in range(0, len(terms), 2)]
        terms = pairs
    total = terms[0]
    tail = total[:, LEAD : LEAD + SPAN]
    tail = jnp.concatenate([tail[h * ROWS : (h + 1) * ROWS] for h in range(H)], axis=1)
    tail = jnp.concatenate([tail, jnp.zeros((ROWS, WIDE - H * SPAN), F32)], axis=1)
    rest = jnp.zeros((16 - ROWS, WIDE), F32)
    table[...] = jnp.concatenate([total[:, :WIDE], tail, rest], axis=0).astype(BF)


def token_kernel(grad_qkv_t, unit, scales, qkv_w, order_t, quads, south):
    grad_normed = matmul(grad_qkv_t[...].T.astype(BF), qkv_w[...])
    inverse = scales[:WT]
    scaled = grad_normed * scales[WT : WT + 1]
    first = jnp.sum(scaled, axis=-1, keepdims=True) * (1.0 / C)
    second = jnp.sum(scaled * unit[...], axis=-1, keepdims=True) * (1.0 / C)
    grad_x = inverse * (scaled - first - unit[...] * second)
    every = matmul(order_t[...], grad_x.astype(BF))
    quads[...] = every[: 2 * QUAD].astype(BF)
    south[...] = folded(every[2 * QUAD :]).astype(BF)


def east_kernel(quads, south, east):
    corner = unfolded(south[...].astype(F32))[QUAD:]
    east[...] = folded(jnp.concatenate([quads[QUAD:].astype(F32), corner], axis=0)).astype(BF)


def finish_kernel(dy, quads, south, east, out, out_s, sem):
    gap = jnp.zeros((4, C), F32)
    lon_halo = unfolded(east[...].astype(F32))
    lat_halo = unfolded(south[...].astype(F32))[:QUAD]
    mine = quads[:QUAD].astype(F32)
    levels = []
    for z in range(WZ):
        rows = []
        for a in range(WA):
            at = (z * SA + a % SA) * 8
            low = lon_halo[at : at + 8] if a >= SA else lon_halo[QUAD + at : QUAD + at + 8]
            high = mine[at : at + 8] if a >= SA else lat_halo[at : at + 8]
            low, high = jnp.concatenate([low, gap]), jnp.concatenate([gap, high])
            rows.append(dy[z, a].astype(F32) + low + high)
        levels.append(jnp.concatenate(rows, axis=0))
    out_s[...] = jnp.stack(levels, axis=1).astype(BF)
    copy = pltpu.make_async_copy(out_s, out, sem)
    copy.start()
    copy.wait()


def widened(rows):
    return jnp.concatenate([rows, jnp.zeros((rows.shape[0], WIDE - C), F32)], axis=1)


def chip_index():
    return lax.div(lax.axis_index("lon"), 2)


def plane_kernel(keep, got, gain_sum, table, mine, to_dp, to_lon, to_both):
    rows = keep.shape[0] // 4

    def piece(other_dp, other_chip):
        dp = dp_index() if not other_dp else 1 - dp_index()
        chip = chip_index() if not other_chip else 1 - chip_index()
        at = pl.ds(pl.multiple_of((2 * dp + chip) * rows, 8), rows)
        return keep[at, :] + got[at, :].astype(F32)

    mine[...] = piece(False, False)
    to_dp[...] = jnp.concatenate(
        [piece(True, False), widened(gain_sum[...]), table[...].astype(F32)], axis=0
    ).astype(BF)
    to_lon[...] = piece(False, True).astype(BF)
    to_both[...] = piece(True, True).astype(BF)


def plane_sum_kernel(mine, sent, from_both, from_dp, from_lon, halo, out, table):
    rows = mine.shape[0]
    got = from_dp[...].astype(F32)
    dense = mine[...] + got[:rows] + from_lon[...].astype(F32) + from_both[...].astype(F32)
    shared = sent[...].astype(F32)[rows:] + got[rows:]
    out[...] = jnp.concatenate([dense, shared[:8], halo[...].astype(F32)], axis=0).astype(BF)
    table[...] = shared[8:].astype(BF)


def sum_kernel(sent, got, out):
    out[...] = (sent[...].astype(F32) + got[...].astype(F32)).astype(BF)


def relay_kernel(sent, got, out):
    sent, got = sent[...].astype(F32), got[...].astype(F32)
    rows = sent.shape[0] - HALO
    out[...] = jnp.concatenate([sent[:rows] + got[:rows], sent[rows:]], axis=0).astype(BF)


def lon_kernel(sent, got, before, quads, out, south, east):
    sent, got = sent[...].astype(F32), got[...].astype(F32)
    rows = sent.shape[0] - HALO
    halo = jnp.where(
        lax.rem(lax.axis_index("lat"), 2) == 1, before[...].astype(F32)[rows:], got[rows:]
    )
    south[...] = halo.astype(BF)
    corner = unfolded(halo)[QUAD:]
    halo = folded(jnp.concatenate([quads[QUAD:].astype(F32), corner], axis=0))
    east[...] = halo.astype(BF)
    out[...] = jnp.concatenate([sent[:rows] + got[:rows], halo], axis=0).astype(BF)


def join_kernel(sent, got, out):
    sent, got = sent[...].astype(F32), got[...].astype(F32)
    rows = sent.shape[0] - HALO - 8
    first = chip_index() == 0
    low = jnp.where(first, sent[:rows], got[:rows])
    high = jnp.where(first, got[:rows], sent[:rows])
    gain_sum = sent[rows : rows + 8] + got[rows : rows + 8]
    out[...] = jnp.concatenate([low, high, gain_sum], axis=0).astype(BF)


def choose_kernel(got, earlier, out):
    rows = earlier.shape[0] - HALO
    earlier = earlier[...].astype(F32)[rows:]
    odd = lax.rem(lax.axis_index("lon"), 2) == 1
    out[...] = jnp.where(odd, got[...].astype(F32), earlier).astype(BF)


def table_rows_kernel(table_sent, table_got, out):
    table = table_sent[...].astype(F32) + table_got[...].astype(F32)
    count = H * ROWS
    tail = table[count : count + ROWS]
    tail = jnp.concatenate([tail[:, h * SPAN : (h + 1) * SPAN] for h in range(H)], axis=0)
    table = jnp.concatenate([table[:count, :LEAD], tail], axis=1)
    for h in range(H):
        rows = [table[h * ROWS + a : h * ROWS + a + 1] for a in range(ROWS)]
        out[h] = jnp.concatenate(rows, axis=1)


def last_kernel(
    sent, got, table, qkv_out, proj_out, gain_out, table_out, dense_s, gain_s, sems
):
    first = pltpu.make_async_copy(table, table_out, sems.at[3])
    first.start()
    sent, got = sent[...].astype(F32), got[...].astype(F32)
    rows = (sent.shape[0] - 8) // 2
    size = 4 * rows // 3
    gain_sum = sent[2 * rows : 2 * rows + 1] + got[2 * rows : 2 * rows + 1]
    gain_s[...] = jnp.where(dp_index() == 0, gain_sum[:, : C // 2], gain_sum[:, C // 2 : C])
    for side, value in ((side_index(), sent), (1 - side_index(), got)):
        for p in range(2):
            at = pl.ds(pl.multiple_of((2 * side + p) * size, 16), size)
            dense_s[at, :] = unfolded(value[p * rows : (p + 1) * rows])
    copies = [
        pltpu.make_async_copy(dense_s.at[: 3 * size], qkv_out, sems.at[0]),
        pltpu.make_async_copy(dense_s.at[3 * size :], proj_out, sems.at[1]),
        pltpu.make_async_copy(gain_s, gain_out, sems.at[2]),
    ]
    for copy in copies:
        copy.start()
    for copy in copies + [first]:
        copy.wait()


def call(kernel, outs, scratch=(), specs=None, flops=1000000, nbytes=1000000, out_specs=None):
    return pl.pallas_call(
        kernel,
        out_shape=outs,
        in_specs=specs,
        out_specs=jax.tree.map(lambda _: VMEM, outs) if out_specs is None else out_specs,
        scratch_shapes=list(scratch),
        compiler_params=pltpu.CompilerParams(vmem_limit_bytes=24 << 20),
        cost_estimate=pl.CostEstimate(flops=flops, bytes_accessed=nbytes, transcendentals=0),
    )


def shaped(rows, cols, dtype):
    return jax.ShapeDtypeStruct((rows, cols), dtype)


def exchanged(value, axis, flip):
    count = lax.axis_size(axis)
    return lax.ppermute(value, axis, [(i, i ^ flip) for i in range(count)])


def exchanged_both(value):
    pairs = [(2 * i + k, 2 * (i ^ 3) + (1 - k)) for i in range(4) for k in range(2)]
    return lax.ppermute(value, ("lon", "dp"), pairs)


def tied(*values):
    return lax.optimization_barrier(values)


def passed_along(value, axis, steps):
    count = lax.axis_size(axis)
    return lax.ppermute(value, axis, [(i, (i + steps) % count) for i in range(count)])


def passed_diagonally(value, steps):
    rows, cols = lax.axis_size("lon"), lax.axis_size("lat")
    pairs = [
        (i * cols + j, ((i + steps) % rows) * cols + (j + steps) % cols)
        for i in range(rows)
        for j in range(cols)
    ]
    return lax.ppermute(value, ("lon", "lat"), pairs)


def body(tokens, grad_out, qkv_weight, proj_weight, norm_gain, bias_table):
    parts = lax.axis_size("dp")
    lon_count, lat_count = lax.axis_size("lon"), lax.axis_size("lat")
    fast = (lon_count, lat_count, parts) == (4, 4, 2)
    n_qkv, n_proj = 3 * C // parts, C // parts
    each = n_qkv + n_proj
    half = each // 2
    tok = tokens.reshape(WZ, WA, WL, C)
    dy = grad_out.reshape(WZ, WA, WL, C)

    strips = [shaped(HALO, WIDE, BF)] * 3
    dense, east, south, corner = call(
        functools.partial(pack_kernel, parts), [shaped(each + 16, C, BF)] + strips, specs=[VMEM] * 5
    )(tok, dy, qkv_weight, proj_weight, norm_gain.reshape(1, n_proj))
    gathered = [dense] + [passed_along(dense, "dp", -k) for k in range(1, parts)]
    south = passed_along(south, "lat", -1)
    corner = passed_diagonally(corner, -1)
    east = passed_along(east, "lon", -1)
    bias = call(
        bias_kernel,
        jax.ShapeDtypeStruct((2, H * WT, 128), F32),
        specs=[VMEM],
        flops=200000000,
    )(bias_table.reshape(H * ROWS, ROWS * SPAN))
    order = token_order()
    packed = parts * 3 * half // 4
    outs = [
        shaped(packed, WIDE, BF),
        shaped(packed, WIDE, F32),
        shaped(8, C, F32),
        jax.ShapeDtypeStruct((2, H * WT, 128), F32),
        shaped(3 * C, WT, F32),
        shaped(WT, C, F32),
        shaped(WT + 16, C, F32),
        shaped(3 * C, C, BF),
    ]
    scratch = [pltpu.VMEM((C, C), BF), pltpu.VMEM((4 * C, C), F32)]
    send, keep, gain_sum, scores_grad, grad_qkv, unit, scales, qkv_full = call(
        functools.partial(main_kernel, parts, 2 if fast else 1),
        outs,
        scratch,
        specs=[VMEM] * (7 + parts),
    )(south, corner, east, tok, dy, bias, jnp.asarray(order, BF), *gathered)
    if fast:
        got = exchanged(send, "lon", 1)
    table = call(table_kernel, shaped(TABLE, WIDE, BF), specs=[VMEM], flops=200000000)(scores_grad)
    if fast:
        piece = packed // 4
        mine, sent, to_lon, to_both = call(
            plane_kernel,
            [
                shaped(piece, WIDE, F32),
                shaped(piece + 8 + TABLE, WIDE, BF),
                shaped(piece, WIDE, BF),
                shaped(piece, WIDE, BF),
            ],
            specs=[VMEM] * 4,
        )(keep, got, gain_sum, table)
        from_both = exchanged_both(to_both)
        got = exchanged(sent, "dp", 1)
        from_lon = exchanged(to_lon, "lon", 3)
    quads, south = call(
        token_kernel,
        [shaped(2 * QUAD, C, BF), shaped(HALO, WIDE, BF)],
        specs=[VMEM] * 5,
        flops=100000000,
    )(grad_qkv, unit, scales, qkv_full, jnp.asarray(order.T, BF))
    if fast:
        lat_shape = shaped(piece + 8 + HALO, WIDE, BF)
        table_shape = shaped(TABLE, WIDE, BF)
        halo_shape = shaped(HALO, WIDE, BF)
        sent, table = call(plane_sum_kernel, [lat_shape, table_shape], specs=[VMEM] * 6)(
            mine, sent, from_both, got, from_lon, south
        )
        before = exchanged(sent, "lat", 1)
        sent = call(relay_kernel, lat_shape, specs=[VMEM] * 2)(sent, before)
        sent, table = tied(sent, table)
        got = exchanged(sent, "lat", 3)
        table_got = exchanged(table, "lon", 3)
        sent, south, east = call(
            lon_kernel, [lat_shape, halo_shape, halo_shape], specs=[VMEM] * 4
        )(sent, got, before, quads)
        sent, table_got = tied(sent, table_got)
        got = exchanged(sent, "lon", 3)
        table = call(sum_kernel, table_shape, specs=[VMEM] * 2)(table, table_got)
        table_got = exchanged(table, "lon", 1)
        east_got = exchanged(east, "lon", 1)
        east = call(choose_kernel, halo_shape, specs=[VMEM] * 2)(east_got, got)
    else:
        south = passed_along(south, "lat", 1)
        east = call(east_kernel, shaped(HALO, WIDE, BF), specs=[VMEM] * 2)(quads, south)
        east = passed_along(east, "lon", 1)
    hbm = pl.BlockSpec(memory_space=pltpu.HBM)
    tile = (WA * WL, WZ, C)
    finish = call(
        finish_kernel,
        jax.ShapeDtypeStruct(tile, BF),
        [pltpu.VMEM(tile, BF), pltpu.SemaphoreType.DMA],
        specs=[VMEM] * 4,
        out_specs=hbm,
    )

    def tokens_of(columns):
        return columns.reshape(WA, WL, WZ, C).transpose(2, 0, 1, 3)[None]

    if fast:
        sent = call(join_kernel, shaped(2 * piece + 8, WIDE, BF), specs=[VMEM] * 2)(sent, got)
        sent, table_got, east = tied(sent, table_got, east)
        got = exchanged(sent, "lon", 1)
        grad_tokens = finish(dy, quads, south, east)
        table = call(
            table_rows_kernel, jax.ShapeDtypeStruct((H, 1, POS), F32), specs=[VMEM] * 2
        )(table, table_got)
        got, grad_tokens, table = tied(got, grad_tokens, table)
        grad_tokens = tokens_of(grad_tokens)
        grad_qkv_w, grad_proj, grad_gain, grad_table = call(
            last_kernel,
            [
                shaped(n_qkv, C, F32),
                shaped(n_proj, C, F32),
                shaped(1, n_proj, F32),
                jax.ShapeDtypeStruct((H, 1, POS), F32),
            ],
            [
                pltpu.VMEM((each, C), F32),
                pltpu.VMEM((1, n_proj), F32),
                pltpu.SemaphoreType.DMA((4,)),
            ],
            specs=[VMEM] * 3,
            out_specs=[hbm] * 4,
        )(sent, got, table)
        grad_gain, grad_table = grad_gain.reshape(n_proj), grad_table.reshape(1, H, POS)
        return grad_tokens, grad_qkv_w, grad_proj, grad_gain, grad_table
    grad_tokens = tokens_of(finish(dy, quads, south, east))
    pair = jnp.stack([keep, send.astype(F32)]).reshape(2, parts, packed // parts, WIDE)
    pair = jnp.where(side_index() == 0, pair, pair[::-1])
    pair = jax.vmap(jax.vmap(unfolded))(pair)
    dense_sum = lax.psum(pair.transpose(1, 0, 2, 3).reshape(parts * each, C), ("lon", "lat"))
    total = lax.psum_scatter(dense_sum, "dp", scatter_dimension=0, tiled=True)
    grad_gain = lax.psum(gain_sum[0], ("lon", "lat"))
    grad_gain = lax.psum_scatter(grad_gain, "dp", scatter_dimension=0, tiled=True)
    table = lax.psum(table.astype(F32), ("lon", "dp"))
    count = H * ROWS
    tail = table[count : count + ROWS, : H * SPAN].reshape(ROWS, H, SPAN)
    tail = tail.transpose(1, 0, 2).reshape(count, SPAN)
    table = jnp.concatenate([table[:count, :LEAD], tail], axis=1)
    return (
        grad_tokens,
        total[:n_qkv],
        total[n_qkv:],
        grad_gain,
        table.reshape(1, H, POS),
    )


def solution(mesh):
    spec = P("dp", None, "lat", "lon", None)
    return jax.shard_map(
        body,
        mesh=mesh,
        in_specs=(spec, spec, P("dp", None), P("dp", None), P("dp"), P("lat", None, None)),
        out_specs=(spec, P("dp", None), P("dp", None), P("dp"), P("lat", None, None)),
        check_vma=False,
    )
```
